128 devices in a mesh: band: 16 (over x, z), head: 4 (over y), dp: 2 (over core).
Axes of the slice: x: 4, y: 4, z: 4, core: 2. Of those that a mesh axis runs over, the one named last changes fastest.
Arguments:
- tokens: bfloat16 [128, 1024, 512], P(('dp', 'band'), None, 'head'), parts along dimension 0, may hold values from -6 to 6
- corner_row: int32 [2048], P('dp'), parts along dimension 0, may hold values from 0 to 62
- corner_col: int32 [2048], P('dp'), parts along dimension 0, may hold values from 0 to 1022
- fraction: float32 [2, 2048], P(None, 'dp'), parts along dimension 1, may hold values from 0 to 1
- w_query: bfloat16 [512, 512], P(None, 'head'), may hold values from -2 to 2
- w_key: bfloat16 [512, 512], P(None, 'head'), may hold values from -2 to 2
- w_value: bfloat16 [512, 512], P(None, 'head'), may hold values from -0.25 to 0.25
- w_out: bfloat16 [512, 512], P('head'), may hold values from -0.25 to 0.25
- conv_kernel: float32 [25, 512], P(None, 'head'), may hold values from -1.25 to 1.25
- norm_gain: float32 [512], replicated, may hold values from 0.1 to 1.9
Outputs:
- mixed: bfloat16 [128, 1024, 512], P(('dp', 'band'), None, 'head'), parts along dimension 0
The draws below stay inside these ranges and needn't reach their ends.
There are 2 independent parts, one for each index of `dp`. The reference program is written for one: setup_inputs(seed, part) draws one part's arguments, and reference() takes and returns one part's arrays. A program takes and returns all parts, laid end to end along the dimension named above; an argument that names none is the same for every part. Nothing has to cross between parts.
All inputs are finite; a program needn't handle non-finite values.
Results may differ from the reference program's by a relative error of at most 0.029.
Values may be sent and summed in bfloat16 or wider, within the bound.
No kernel may reach another device: no remote copies, remote signals or barrier semaphores. Data moves between devices by JAX's collectives and lax.ppermute only.
A program may use at most 64 MiB of HBM per device.

```python
import math
import jax
import jax.numpy as jnp
import numpy as np
from jax import lax

D = 512
HEADS = 16
KER = 5
POINTS = 1024
W = 1024
HEAD_DIM = 32
H = 64
N_HEAD = 4


def paired_weight(key, salt):
    own = jax.random.normal(jax.random.fold_in(key, salt), (D, D), jnp.float32)
    values = own / D ** 0.5
    return jnp.clip(values, -2.0, 2.0).astype(jnp.bfloat16)


def draw_w_query(key, part):
    return paired_weight(key, 211)


def draw_w_key(key, part):
    return paired_weight(key, 307)


def plant(array, stream_key, smallest, top_value):
    extent = array.shape
    spot = [jax.random.randint(jax.random.fold_in(stream_key, axis), (), 0, extent[axis]) for axis in range(len(extent))]
    array = array.at[tuple(spot)].set(smallest)
    longest = extent.index(max(extent))
    spot[longest] = (spot[longest] + 1) % extent[longest]
    return array.at[tuple(spot)].set(top_value)


def steps_of(own_key, extent, cuts, low, largest):
    gain, own = 1.0, jax.random.fold_in(own_key, 6)
    for dim, blocks in cuts:
        draws = jnp.exp(jax.random.uniform(jax.random.fold_in(own, dim), (blocks,), jnp.float32, low / len(cuts), largest / len(cuts)))
        gain = gain * jnp.repeat(draws, extent[dim] // blocks).reshape([-1 if axis == dim else 1 for axis in range(len(extent))])
    return gain


def rank_table(amount, skew):
    loads = [(1 << 20) // math.isqrt(rank ** skew) + 1 for rank in range(1, amount + 1)]
    width = 1 + sum(loads) // (1 << 30)
    return np.cumsum(np.array([max(1, weight // width) for weight in loads]))


def ranked(key, dims, amount, lean):
    table = rank_table(amount, lean)
    ticket = jax.random.randint(jax.random.fold_in(key, 1), dims, 0, int(table[amount - 1]))
    standing = jnp.searchsorted(jnp.asarray(table, jnp.int32), ticket, side="right")
    return jax.random.permutation(jax.random.fold_in(key, 2), amount)[standing].astype(jnp.int32)


def scatter_about(rng, dims, scale, limit, split=(), held_as=jnp.bfloat16):
    level = steps_of(rng, dims, split, -0.22, 0.18) if split else 1.0
    values = jax.random.normal(rng, dims, jnp.float32) * scale * level
    return jnp.minimum(jnp.maximum(values, -limit), limit).astype(held_as)


def setup_inputs(seed: int = 0, part: int = 0) -> dict:
    key_list = jax.random.split(jax.random.key(seed), 11)
    part_keys = jax.random.split(jax.random.fold_in(key_list[10], part), 11)
    tokens = scatter_about(part_keys[0], (H, W, D), 1.0, 6.0, ((0, 16), (2, 4)))
    corner_row = plant(ranked(part_keys[1], (POINTS,), H - 1, 2), jax.random.fold_in(part_keys[1], 3), 0, (H - 1) - 1).astype(jnp.int32)
    corner_col = plant(jax.random.randint(part_keys[2], (POINTS,), 0, W - 1), jax.random.fold_in(part_keys[2], 1), 0, (W - 1) - 1).astype(jnp.int32)
    fraction = jnp.clip(jax.random.uniform(part_keys[3], (2, POINTS), jnp.float32, 0.0, 1.0), 0.0, 1.0)
    w_query = draw_w_query(jax.random.fold_in(key_list[10], 71), part)
    w_key = draw_w_key(jax.random.fold_in(key_list[10], 71), part)
    w_value = scatter_about(key_list[6], (D, D), D ** -0.5, 0.25, ((1, 4),))
    w_out = scatter_about(key_list[7], (D, D), D ** -0.5, 0.25, ((0, 4),))
    conv_kernel = scatter_about(key_list[8], (KER * KER, D), (KER * KER) ** -0.5, 1.25, ((1, 4),), jnp.float32)
    norm_gain = jnp.clip(1.0 + 0.18 * jax.random.normal(key_list[9], (D,), jnp.float32), 0.1, 1.9)
    return dict(tokens=tokens, corner_row=corner_row, corner_col=corner_col, fraction=fraction, w_query=w_query, w_key=w_key, w_value=w_value, w_out=w_out, conv_kernel=conv_kernel, norm_gain=norm_gain)


def layer_norm(values, norm_gain):
    values = values.astype(jnp.float32)
    center = lax.optimization_barrier(jnp.mean(values, axis=-1, keepdims=True))
    spread = lax.optimization_barrier(jnp.mean(jnp.square(values - center), axis=-1, keepdims=True))
    return ((values - center) * lax.rsqrt(spread + 1e-05) * norm_gain).astype(jnp.bfloat16)

def reference(tokens, corner_row, corner_col, fraction, w_query, w_key, w_value, w_out, conv_kernel, norm_gain):
    normed = layer_norm(tokens, norm_gain)
    count = H * W
    flat = normed.reshape(count, D)
    query = jnp.dot(flat, w_query, preferred_element_type=jnp.float32).astype(jnp.bfloat16)
    row_top = (1.0 - fraction[0]).astype(jnp.bfloat16).astype(jnp.float32)[:, None]
    row_bottom = fraction[0].astype(jnp.bfloat16).astype(jnp.float32)[:, None]
    col_left = (1.0 - fraction[1]).astype(jnp.bfloat16).astype(jnp.float32)[:, None]
    col_right = fraction[1].astype(jnp.bfloat16).astype(jnp.float32)[:, None]
    grid = normed.astype(jnp.float32)
    inner_top = col_left * grid[corner_row, corner_col] + col_right * grid[corner_row, corner_col + 1]
    inner_bottom = col_left * grid[corner_row + 1, corner_col] + col_right * grid[corner_row + 1, corner_col + 1]
    sampled = (row_top * inner_top + row_bottom * inner_bottom).astype(jnp.bfloat16)
    key = jnp.dot(sampled, w_key, preferred_element_type=jnp.float32).astype(jnp.bfloat16)
    value = jnp.dot(sampled, w_value, preferred_element_type=jnp.float32).astype(jnp.bfloat16)
    key_heads = key.reshape(POINTS, HEADS, HEAD_DIM).astype(jnp.float32)
    value_heads = value.reshape(POINTS, HEADS, HEAD_DIM).astype(jnp.float32)
    block = min(512, count)
    blocks = query.reshape(count // block, block, HEADS, HEAD_DIM)
    scale = 1.0 / HEAD_DIM ** 0.5

    def one_block(part):
        scores = jnp.einsum('qhd,khd->hqk', part.astype(jnp.float32), key_heads) * scale
        top = lax.optimization_barrier(jnp.max(scores, axis=-1, keepdims=True))
        expo = jnp.exp(scores - top)
        probs = (expo / lax.optimization_barrier(jnp.sum(expo, axis=-1, keepdims=True))).astype(jnp.bfloat16)
        out = jnp.einsum('hqk,khd->qhd', probs.astype(jnp.float32), value_heads)
        return out.astype(jnp.bfloat16).reshape(block, D)
    attended = lax.map(one_block, blocks).reshape(count, D)
    group = D // N_HEAD
    projected = jnp.zeros((count, D), jnp.float32)
    for index in range(N_HEAD):
        partial_sum = jnp.dot(attended[:, index * group:(index + 1) * group], w_out[index * group:(index + 1) * group], preferred_element_type=jnp.float32)
        partial_sum = lax.optimization_barrier(partial_sum.astype(jnp.bfloat16)).astype(jnp.float32)
        projected = projected + partial_sum
    margin = KER // 2
    padded = jnp.pad(grid, ((margin, margin), (margin, margin), (0, 0)))
    local = jnp.zeros((H, W, D), jnp.float32)
    for first in range(KER):
        for second in range(KER):
            local = local + conv_kernel[first * KER + second] * padded[first:first + H, second:second + W]
    total = tokens.astype(jnp.float32) + projected.reshape(H, W, D) + local
    return total.astype(jnp.bfloat16)
```

```python
import functools

import jax
import jax.numpy as jnp
from jax import lax
from jax.experimental import pallas as pl
from jax.experimental.pallas import tpu as pltpu
from jax.sharding import PartitionSpec as P


HEADS = 16
KER = 5
EPS = 1e-05
F32 = jnp.float32
BF = jnp.bfloat16
ROW_BY_ROW = (((1,), (1,)), ((), ()))
COLUMN_BY_COLUMN = (((0,), (0,)), ((), ()))


def from_everyone(x, axis):
    copies = jnp.broadcast_to(x, (lax.axis_size(axis), *x.shape))
    return lax.all_to_all(copies, axis, split_axis=0, concat_axis=0, tiled=True)


def split_in_two(x):
    high = x.astype(BF)
    return high, (x - high.astype(F32)).astype(BF)


def split_in_three(x):
    high = x.astype(BF)
    rest = x - high.astype(F32)
    middle = rest.astype(BF)
    return high, middle, (rest - middle.astype(F32)).astype(BF)


def moments_kernel(tokens_ref, out_ref):
    rows, columns, channels = tokens_ref.shape
    ones = jnp.ones((8, channels), BF)
    average = jnp.full((channels, channels), 1.0 / channels, BF)
    for row in range(rows):
        block = tokens_ref[row]
        center = jnp.dot(block, average, preferred_element_type=F32)
        square = jnp.square(block.astype(F32) - center)
        high, low = split_in_two(square)
        total = lax.dot_general(ones, block, ROW_BY_ROW, preferred_element_type=F32)
        spread = lax.dot_general(ones, high, ROW_BY_ROW, preferred_element_type=F32)
        spread = spread + lax.dot_general(ones, low, ROW_BY_ROW, preferred_element_type=F32)
        at = pl.ds(row * columns, columns)
        for copy in range(out_ref.shape[0]):
            out_ref[copy, 0:1, at] = total[0:1]
            out_ref[copy, 1:2, at] = spread[0:1]


def local_moments(tokens, copies):
    rows, columns, _ = tokens.shape
    return pl.pallas_call(
        moments_kernel,
        out_shape=jax.ShapeDtypeStruct((copies, 2, rows * columns), F32),
        cost_estimate=pl.CostEstimate(flops=10**9, bytes_accessed=2**20, transcendentals=0),
        name="moments",
    )(tokens)


def normalize_sample_kernel(
    tokens_ref, moments_ref, gain_ref, table_ref, weight_ref, normed_ref, sampled_ref, planes
):
    rows, columns, channels = tokens_ref.shape
    devices = moments_ref.shape[0]
    sums = [moments_ref[d, 0:1, :] for d in range(devices)]
    width = channels * devices
    center = functools.reduce(jnp.add, sums) * (1.0 / width)
    spread = functools.reduce(jnp.add, [moments_ref[d, 1:2, :] for d in range(devices)])
    for d in range(devices):
        spread = spread + channels * jnp.square(sums[d] * (1.0 / channels) - center)
    factor = lax.rsqrt(spread * (1.0 / width) + EPS)
    pieces = [*split_in_three(center), *split_in_three(factor)]
    pieces += [jnp.zeros_like(pieces[0])] * 10
    stacked = jnp.concatenate([p.astype(F32) for p in pieces], axis=0).astype(BF)
    piece = lax.broadcasted_iota(jnp.int32, (16, 2 * channels), 0)
    lane = lax.broadcasted_iota(jnp.int32, (16, 2 * channels), 1)
    pick = jnp.where((piece < 6) & (piece // 3 == lane // channels), 1.0, 0.0).astype(BF)
    for row in range(rows):
        part = stacked[:, row * columns : (row + 1) * columns]
        spreadout = lax.dot_general(part, pick, COLUMN_BY_COLUMN, preferred_element_type=F32)
        values = tokens_ref[row].astype(F32) - spreadout[:, :channels]
        values = (values * spreadout[:, channels:] * gain_ref[...]).astype(BF)
        normed_ref[row] = values
        planes[:, row * channels : (row + 1) * channels] = values
    inner = jnp.dot(table_ref[...], planes[...], preferred_element_type=F32)
    total = None
    for row in range(rows):
        at = slice(row * channels, (row + 1) * channels)
        part = weight_ref[:, at].astype(F32) * inner[:, at]
        total = part if total is None else total + part
    sampled_ref[...] = total.astype(BF)


def normalize_and_sample(tokens, moments, gain, table, weight):
    rows, columns, channels = tokens.shape
    points = table.shape[0]
    return pl.pallas_call(
        normalize_sample_kernel,
        out_shape=(
            jax.ShapeDtypeStruct(tokens.shape, BF),
            jax.ShapeDtypeStruct((points, channels), BF),
        ),
        scratch_shapes=[pltpu.VMEM((columns, rows * channels), BF)],
        cost_estimate=pl.CostEstimate(flops=2 * 10**9, bytes_accessed=6 * 2**20, transcendentals=0),
        name="normalize_sample",
    )(tokens, moments, gain, table, weight)


def query_kernel(scale, place_ref, *refs):
    *row_refs, gain_ref, weight_ref, out_ref = refs
    groups = len(row_refs)
    channels = row_refs[0].shape[1]
    width = groups * channels
    parts = [ref[...].astype(F32) for ref in row_refs]
    center = sum(jnp.sum(p, axis=1, keepdims=True) for p in parts) * (1.0 / width)
    parts = [p - center for p in parts]
    spread = sum(jnp.sum(jnp.square(p), axis=1, keepdims=True) for p in parts) * (1.0 / width)
    factor = lax.rsqrt(spread + EPS)
    normed, lines = [], []
    for distance, part in enumerate(parts):
        source = lax.rem(place_ref[0] + (groups - distance), groups)
        normed.append((part * factor * gain_ref[pl.ds(source, 1), :]).astype(BF))
        line = pl.ds(pl.multiple_of(source * channels, channels), channels)
        lines.append(jnp.concatenate([weight_ref[g, line, :] for g in range(groups)], axis=1))
    normed = jnp.concatenate(normed, axis=1)
    weight = jnp.concatenate(lines, axis=0)
    query = jnp.dot(normed, weight, preferred_element_type=F32) * scale
    for g in range(groups):
        out_ref[g] = query[:, g * channels : (g + 1) * channels].astype(BF)


def query_of(place, row, gain, weight, columns, scale):
    groups = len(row)
    channels = row[0].shape[1]
    depth = weight.shape[2]
    block = 256
    return pl.pallas_call(
        functools.partial(query_kernel, scale),
        grid_spec=pltpu.PrefetchScalarGridSpec(
            num_scalar_prefetch=1,
            grid=(columns // block,),
            in_specs=[pl.BlockSpec((block, channels), lambda i, place: (i, 0))] * groups
            + [
                pl.BlockSpec(gain.shape, lambda i, place: (0, 0)),
                pl.BlockSpec((groups, None, depth, channels), lambda i, place: (0, 0, 0, 0)),
            ],
            out_specs=pl.BlockSpec((groups, block, channels), lambda i, place: (0, i, 0)),
        ),
        out_shape=jax.ShapeDtypeStruct((groups, columns, channels), BF),
        cost_estimate=pl.CostEstimate(flops=2 * 10**9, bytes_accessed=3 * 2**20, transcendentals=0),
        name="query",
    )(place, *row, gain, weight)


def key_value_kernel(blocks_ref, key_weight_ref, value_weight_ref, key_ref, value_ref, sampled):
    bands, groups, share, channels = blocks_ref.shape
    for b in range(bands):
        for g in range(groups):
            sampled[b * share : (b + 1) * share, g * channels : (g + 1) * channels] = blocks_ref[b, g]
    for g in range(groups):
        weight = jnp.concatenate([key_weight_ref[g], value_weight_ref[g]], axis=1)
        product = jnp.dot(sampled[...], weight, preferred_element_type=F32)
        key_ref[g] = product[:, :channels].astype(BF)
        value_ref[g] = product[:, channels:].astype(BF)


def keys_and_values(blocks, early, late):
    bands, groups, share, channels = blocks.shape
    depth = early.shape[2]
    out = jax.ShapeDtypeStruct((groups, bands * share, channels), BF)
    whole = pl.BlockSpec((groups, bands * share, channels), lambda i: (0, 0, 0))
    return pl.pallas_call(
        key_value_kernel,
        grid=(1,),
        in_specs=[
            pl.BlockSpec(blocks.shape, lambda i: (0, 0, 0, 0)),
            pl.BlockSpec((groups, None, depth, channels), lambda i: (0, 1, 0, 0)),
            pl.BlockSpec((groups, None, depth, channels), lambda i: (0, 0, 0, 0)),
        ],
        out_specs=(whole, whole),
        out_shape=(out, out),
        scratch_shapes=[pltpu.VMEM((bands * share, depth), BF)],
        cost_estimate=pl.CostEstimate(flops=2 * 10**9, bytes_accessed=4 * 2**20, transcendentals=0),
        name="key_value",
    )(blocks, early, late)


def attend_kernel(
    per_group, query_ref, key_ref, value_ref, weight_ref, out_ref, attended, joined
):
    groups, block, channels = query_ref.shape
    head = lax.broadcasted_iota(jnp.int32, (1, channels), 1) // (channels // per_group)
    zero = jnp.zeros((), BF)

    @pl.when(pl.program_id(0) == 0)
    def _():
        for g in range(groups):
            lines = slice(g * channels, (g + 1) * channels)
            for j in range(groups):
                at = slice(j * channels, (j + 1) * channels)
                joined[lines, at] = weight_ref[g, at, :]

    one = jnp.ones((), BF)
    for g in range(groups):
        total = jnp.zeros((block, 2 * channels), F32)
        for h in range(per_group):
            key = jnp.where(head == h, key_ref[g], zero)
            scores = lax.dot_general(query_ref[g], key, ROW_BY_ROW, preferred_element_type=F32)
            top = jnp.max(scores, axis=-1, keepdims=True)
            probs = jnp.exp2(scores - top).astype(BF)
            value = jnp.where(head == h, value_ref[g], zero)
            ones = jnp.broadcast_to(jnp.where(head == h, one, zero), value.shape)
            both = jnp.concatenate([value, ones], axis=1)
            total = total + jnp.dot(probs, both, preferred_element_type=F32)
        at = slice(g * channels, (g + 1) * channels)
        attended[:, at] = (total[:, :channels] / total[:, channels:]).astype(BF)
    projected = jnp.dot(attended[...], joined[...], preferred_element_type=F32)
    for g in range(groups):
        out_ref[g] = projected[:, g * channels : (g + 1) * channels].astype(BF)


def attend_and_project(query, key, value, weight, first, count):
    groups, _, channels = query.shape
    points = key.shape[1]
    block = 256
    width = groups * channels
    start = first // block
    whole = pl.BlockSpec(key.shape, lambda i: (0, 0, 0))
    return pl.pallas_call(
        functools.partial(attend_kernel, HEADS // groups),
        grid=(count // block,),
        in_specs=[
            pl.BlockSpec((groups, block, channels), lambda i: (0, i + start, 0)),
            whole,
            whole,
            pl.BlockSpec((groups, None, width, channels), lambda i: (0, 1, 0, 0)),
        ],
        out_specs=pl.BlockSpec((groups, block, channels), lambda i: (0, i, 0)),
        out_shape=jax.ShapeDtypeStruct((groups, count, channels), BF),
        scratch_shapes=[pltpu.VMEM((block, width), BF), pltpu.VMEM((width, width), BF)],
        cost_estimate=pl.CostEstimate(
            flops=4 * count * points * width, bytes_accessed=4 * 2**20, transcendentals=0
        ),
        name="attend",
    )(query, key, value, weight)


def convolve_kernel(low_ref, normed_ref, high_ref, tokens_ref, taps_ref, out_ref, padded):
    rows, columns, channels = normed_ref.shape
    margin = KER // 2
    pad = 8
    padded[:, 0:pad, :] = jnp.zeros((rows + 2 * margin, pad, channels), F32)
    padded[:, pad + columns :, :] = jnp.zeros((rows + 2 * margin, pad, channels), F32)
    padded[0:margin, pad : pad + columns, :] = low_ref[...].astype(F32)
    padded[margin : margin + rows, pad : pad + columns, :] = normed_ref[...].astype(F32)
    padded[margin + rows :, pad : pad + columns, :] = high_ref[...].astype(F32)
    taps = taps_ref[...]
    strip = 8

    def one_strip(index, carry):
        start = pl.multiple_of(index * strip, strip)
        totals = [tokens_ref[r, pl.ds(start, strip), :].astype(F32) for r in range(rows)]
        for second in range(KER):
            for line in range(rows + 2 * margin):
                values = padded[line, pl.ds(start + pad - margin + second, strip), :]
                for r in range(rows):
                    first = line - r
                    if 0 <= first < KER:
                        tap = first * KER + second
                        totals[r] = totals[r] + taps[tap : tap + 1, :] * values
        for r in range(rows):
            out_ref[r, pl.ds(start, strip), :] = totals[r]
        return carry

    lax.fori_loop(0, columns // strip, one_strip, 0)


def convolve(low, normed, high, tokens, taps):
    rows, columns, channels = normed.shape
    return pl.pallas_call(
        convolve_kernel,
        out_shape=jax.ShapeDtypeStruct(normed.shape, F32),
        scratch_shapes=[pltpu.VMEM((rows + 2 * (KER // 2), columns + 16, channels), F32)],
        cost_estimate=pl.CostEstimate(
            flops=10**9, bytes_accessed=6 * 2**20, transcendentals=0
        ),
        name="convolve",
    )(low, normed, high, tokens, taps)


def column_table(corner_col, col_left, col_right, columns):
    positions = lax.broadcasted_iota(jnp.int32, (1, columns), 1)
    zero = jnp.zeros((), BF)
    left = jnp.where(positions == corner_col[:, None], col_left[:, None], zero)
    right = jnp.where(positions == corner_col[:, None] + 1, col_right[:, None], zero)
    return left + right


def row_weights(corner_row, row_top, row_bottom, band_start, rows, channels):
    grid_rows = band_start + lax.broadcasted_iota(jnp.int32, (1, rows * channels), 1) // channels
    zero = jnp.zeros((), BF)
    top = jnp.where(grid_rows == corner_row[:, None], row_top[:, None], zero)
    bottom = jnp.where(grid_rows == corner_row[:, None] + 1, row_bottom[:, None], zero)
    return top + bottom


def body(
    tokens, corner_row, corner_col, fraction, w_query, w_key, w_value, w_out, conv_kernel, norm_gain
):
    rows, columns, channels = tokens.shape
    groups = lax.axis_size("head")
    bands = lax.axis_size("band")
    width = groups * channels
    points = corner_row.shape[0]
    share = points // bands

    place = lax.axis_index("head")
    core = lax.axis_index("dp")
    moments = local_moments(tokens, groups)
    moments = lax.all_to_all(moments, "head", 0, 0, tiled=True)
    stacked_out = [w_out[:, g * channels : (g + 1) * channels] for g in range(groups)]
    first = jnp.concatenate([w_query, w_key], axis=0)
    second = jnp.concatenate([w_value, *stacked_out], axis=0)
    half = jnp.where(core == 0, first, second)
    bulk = [
        jnp.concatenate(
            [
                lax.dynamic_index_in_dim(
                    tokens, lax.rem(place + distance, groups), 0, keepdims=False
                ),
                half,
            ],
            axis=0,
        )
        for distance in range(1, groups)
    ]
    arrived = []
    for distance in (2, 1, 3):
        ring = [(i, (i + distance) % groups) for i in range(groups)]
        arrived.append((distance, lax.ppermute(bulk[distance - 1], "head", ring)))
    arrived = [block for _, block in sorted(arrived, key=lambda item: item[0])]
    other = [lax.ppermute(a[columns:], "dp", [(0, 1), (1, 0)]) for a in arrived]
    depth = w_query.shape[0]
    early = [first] + [jnp.where(core == 0, a[columns:], o) for a, o in zip(arrived, other)]
    late = [second] + [jnp.where(core == 0, o, a[columns:]) for a, o in zip(arrived, other)]
    early = jnp.stack(early).reshape(groups, 2, depth, channels)
    late = jnp.stack(late).reshape(groups, 2, depth, channels)
    own_row = lax.dynamic_index_in_dim(tokens, place, 0, keepdims=False)

    row_top = (1.0 - fraction[0]).astype(BF)
    row_bottom = fraction[0].astype(BF)
    col_left = (1.0 - fraction[1]).astype(BF)
    col_right = fraction[1].astype(BF)
    table = column_table(corner_col, col_left, col_right, columns)
    weight = row_weights(
        corner_row, row_top, row_bottom, lax.axis_index("band") * rows, rows, channels
    )
    gain = norm_gain.reshape(groups, channels)
    gain_here = lax.dynamic_slice_in_dim(gain, lax.axis_index("head"), 1, 0)
    normed, partial = normalize_and_sample(tokens, moments, gain_here, table, weight)

    parts = lax.all_to_all(partial.reshape(bands, share, channels), "band", 0, 0, tiled=True)
    forward = [(i, i + 1) for i in range(bands - 1)]
    backward = [(target, source) for source, target in forward]
    margin = KER // 2
    low = lax.ppermute(normed[rows - margin :], "band", forward)
    high = lax.ppermute(normed[:margin], "band", backward)
    piece = jnp.sum(parts.astype(F32), axis=0).astype(BF)
    blocks = from_everyone(piece, ("band", "head")).reshape(bands, groups, share, channels)

    size = width // HEADS
    scale = 1.4426950408889634 / size**0.5
    query = query_of(place.reshape(1), [own_row, *arrived], gain, early, columns, scale)
    base = convolve(low, normed, high, tokens, conv_kernel)
    key, value = keys_and_values(blocks, early, late)
    chunks = 2
    count = columns // chunks
    returned = []
    for chunk in range(chunks):
        projected = attend_and_project(query, key, value, late, chunk * count, count)
        returned.append(lax.all_to_all(projected, "head", 0, 0, tiled=True))
    projected = jnp.concatenate(returned, axis=1)
    return (base + projected.astype(F32)).astype(BF)


def solution(mesh):
    return jax.shard_map(
        body,
        mesh=mesh,
        in_specs=(
            P(("dp", "band"), None, "head"),
            P("dp"),
            P("dp"),
            P(None, "dp"),
            P(None, "head"),
            P(None, "head"),
            P(None, "head"),
            P("head", None),
            P(None, "head"),
            P(),
        ),
        out_specs=P(("dp", "band"), None, "head"),
        check_vma=False,
    )
```

```python
import functools

import jax
import jax.numpy as jnp
from jax import lax
from jax.experimental import pallas as pl
from jax.experimental.pallas import tpu as pltpu
from jax.sharding import PartitionSpec as P


HEADS = 16
KER = 5
EPS = 1e-05
F32 = jnp.float32
BF = jnp.bfloat16
ROW_BY_ROW = (((1,), (1,)), ((), ()))
COLUMN_BY_COLUMN = (((0,), (0,)), ((), ()))


def split_in_three(x):
    high = x.astype(BF)
    rest = x - high.astype(F32)
    middle = rest.astype(BF)
    return high, middle, (rest - middle.astype(F32)).astype(BF)


def moments_kernel(tokens_ref, out_ref):
    rows, columns, channels = tokens_ref.shape
    half = lax.broadcasted_iota(jnp.int32, (8, 2 * channels), 1) // channels
    pick = jnp.where(half == lax.broadcasted_iota(jnp.int32, (8, 2 * channels), 0), 1.0, 0.0)
    pick = pick.astype(BF)
    average = jnp.full((channels, channels), 1.0 / channels, BF)
    for row in range(rows):
        block = tokens_ref[row]
        center = jnp.dot(block, average, preferred_element_type=F32)
        square = jnp.square(block.astype(F32) - center).astype(BF)
        both = jnp.concatenate([block, square], axis=1)
        facts = lax.dot_general(pick, both, ROW_BY_ROW, preferred_element_type=F32)
        at = pl.ds(row * columns, columns)
        for copy in range(out_ref.shape[0]):
            out_ref[copy, :, at] = facts[0:2]


def local_moments(tokens, copies):
    rows, columns, _ = tokens.shape
    return pl.pallas_call(
        moments_kernel,
        out_shape=jax.ShapeDtypeStruct((copies, 2, rows * columns), F32),
        cost_estimate=pl.CostEstimate(flops=10**9, bytes_accessed=2**20, transcendentals=0),
        name="moments",
    )(tokens)


def tables_kernel(band_ref, row_ref, column_ref, fraction_ref, table_ref, weight_ref):
    _, columns = table_ref.shape
    rows = weight_ref.shape[1] // 128
    lines = row_ref[...]
    start = band_ref[0] * rows
    column = column_ref[...]
    vertical = fraction_ref[0:1, :]
    horizontal = fraction_ref[1:2, :]
    top = (1.0 - vertical).astype(BF).astype(F32)
    bottom = vertical.astype(BF).astype(F32)
    coarse = (column // 8) * 8
    facts = [
        coarse.astype(F32),
        (column - coarse).astype(F32),
        (1.0 - horizontal).astype(BF).astype(F32),
        horizontal.astype(BF).astype(F32),
    ]
    for r in range(rows):
        here = jnp.where(lines == start + r, top, 0.0)
        facts.append(here + jnp.where(lines + 1 == start + r, bottom, 0.0))
    facts += [jnp.zeros_like(facts[0])] * (16 - len(facts))
    facts = jnp.concatenate(facts, axis=0).astype(BF)
    kinds = 3 + rows
    fact = lax.broadcasted_iota(jnp.int32, (16, kinds * 128), 0)
    kind = lax.broadcasted_iota(jnp.int32, (16, kinds * 128), 1) // 128
    pick = (jnp.maximum(fact - 1, 0) == kind) & (fact < kinds + 1)
    spread = lax.dot_general(
        facts,
        jnp.where(pick, 1.0, 0.0).astype(BF),
        COLUMN_BY_COLUMN,
        preferred_element_type=F32,
    )
    weight_ref[...] = spread[:, 3 * 128 :].astype(BF)
    middle = spread[:, :128]
    left, right = spread[:, 128:256], spread[:, 256:384]
    lane = lax.broadcasted_iota(jnp.int32, (1, 128), 1).astype(F32)
    for block in range(columns // 128):
        offset = lane + float(block * 128) - middle
        values = jnp.where(offset == 0.0, left, jnp.where(offset == 1.0, right, 0.0))
        table_ref[:, block * 128 : (block + 1) * 128] = values.astype(BF)


def tables(band, corner_row, corner_col, fraction, columns, rows):
    points = corner_row.shape[0]
    vmem = pl.BlockSpec(memory_space=pltpu.VMEM)
    return pl.pallas_call(
        tables_kernel,
        in_specs=[pl.BlockSpec(memory_space=pltpu.SMEM), vmem, vmem, vmem],
        out_specs=(vmem, vmem),
        out_shape=(
            jax.ShapeDtypeStruct((points, columns), BF),
            jax.ShapeDtypeStruct((points, rows * 128), BF),
        ),
        cost_estimate=pl.CostEstimate(flops=10**9, bytes_accessed=3 * 2**20, transcendentals=0),
        name="tables",
    )(band, corner_row.reshape(1, points), corner_col.reshape(1, points), fraction)


def normalize_sample_kernel(
    place_ref,
    gain_ref,
    tokens_hbm,
    moments_hbm,
    table_hbm,
    weight_hbm,
    normed_hbm,
    low_hbm,
    high_hbm,
    sampled_ref,
    tokens,
    moments,
    table,
    weights,
    normed,
    planes,
    arrive,
    leave,
):
    fetches = []
    for index, (source, target) in enumerate(
        ((moments_hbm, moments), (tokens_hbm, tokens), (table_hbm, table), (weight_hbm, weights))
    ):
        fetches.append(pltpu.make_async_copy(source, target, arrive.at[index]))
        fetches[-1].start()
    rows, columns, channels = tokens.shape
    devices = moments.shape[0]
    fetches[0].wait()
    sums = [moments[d, 0:1, :] for d in range(devices)]
    width = channels * devices
    center = functools.reduce(jnp.add, sums) * (1.0 / width)
    spread = functools.reduce(jnp.add, [moments[d, 1:2, :] for d in range(devices)])
    for d in range(devices):
        spread = spread + channels * jnp.square(sums[d] * (1.0 / channels) - center)
    factor = lax.rsqrt(spread * (1.0 / width) + EPS)
    pieces = [*split_in_three(center), *split_in_three(factor)]
    pieces += [jnp.zeros_like(pieces[0])] * 10
    stacked = jnp.concatenate([p.astype(F32) for p in pieces], axis=0).astype(BF)
    piece = lax.broadcasted_iota(jnp.int32, (16, 2 * channels), 0)
    lane = lax.broadcasted_iota(jnp.int32, (16, 2 * channels), 1)
    pick = jnp.where((piece < 6) & (piece // 3 == lane // channels), 1.0, 0.0).astype(BF)
    gain = gain_ref[pl.ds(place_ref[0], 1), :]
    margin = KER // 2
    fetches[1].wait()
    stores = []

    def send(source, target):
        stores.append(pltpu.make_async_copy(source, target, leave.at[len(stores)]))
        stores[-1].start()

    for row in range(rows):
        part = stacked[:, row * columns : (row + 1) * columns]
        spreadout = lax.dot_general(part, pick, COLUMN_BY_COLUMN, preferred_element_type=F32)
        values = tokens[row].astype(F32) - spreadout[:, :channels]
        values = (values * spreadout[:, channels:] * gain).astype(BF)
        normed[row] = values
        planes[:, row * channels : (row + 1) * channels] = values
    send(normed, normed_hbm)
    send(normed.at[pl.ds(rows - margin, margin)], low_hbm)
    send(normed.at[pl.ds(0, margin)], high_hbm)
    fetches[2].wait()
    inner = jnp.dot(table[...], planes[...], preferred_element_type=F32)
    fetches[3].wait()
    total = None
    for row in range(rows):
        at = slice(row * channels, (row + 1) * channels)
        part = weights[:, at].astype(F32) * inner[:, at]
        total = part if total is None else total + part
    sampled_ref[...] = total.astype(BF)
    for store in stores:
        store.wait()


def normalize_and_sample(place, gain, tokens, moments, table, weight):
    rows, columns, channels = tokens.shape
    points = table.shape[0]
    vmem = pl.BlockSpec(memory_space=pltpu.VMEM)
    anywhere = pl.BlockSpec(memory_space=pl.ANY)
    edge = jax.ShapeDtypeStruct((KER // 2, columns, channels), BF)
    return pl.pallas_call(
        normalize_sample_kernel,
        in_specs=[pl.BlockSpec(memory_space=pltpu.SMEM), vmem] + [anywhere] * 4,
        out_specs=(anywhere, anywhere, anywhere, vmem),
        out_shape=(
            jax.ShapeDtypeStruct(tokens.shape, BF),
            edge,
            edge,
            jax.ShapeDtypeStruct((points, channels), BF),
        ),
        scratch_shapes=[
            pltpu.VMEM(tokens.shape, BF),
            pltpu.VMEM(moments.shape, F32),
            pltpu.VMEM(table.shape, BF),
            pltpu.VMEM(weight.shape, BF),
            pltpu.VMEM(tokens.shape, BF),
            pltpu.VMEM((columns, rows * channels), BF),
            pltpu.SemaphoreType.DMA((4,)),
            pltpu.SemaphoreType.DMA((3,)),
        ],
        cost_estimate=pl.CostEstimate(flops=2 * 10**9, bytes_accessed=6 * 2**20, transcendentals=0),
        name="normalize_sample",
    )(place, gain, tokens, moments, table, weight)


def query_kernel(scale, groups, place_ref, *refs):
    row_refs, refs = refs[:groups], refs[groups:]
    gain_ref, own_ref, *rest = refs
    near_refs, far_refs, (out_ref,) = rest[: groups - 1], rest[groups - 1 : -1], rest[-1:]
    channels = row_refs[0].shape[1]
    width = groups * channels
    place, core = place_ref[0], place_ref[1]
    parts = [ref[...].astype(F32) for ref in row_refs]
    center = sum(jnp.sum(p, axis=1, keepdims=True) for p in parts) * (1.0 / width)
    parts = [p - center for p in parts]
    spread = sum(jnp.sum(jnp.square(p), axis=1, keepdims=True) for p in parts) * (1.0 / width)
    factor = lax.rsqrt(spread + EPS)
    normed, lines = [], []
    for distance, part in enumerate(parts):
        source = lax.rem(place + (groups - distance), groups)
        normed.append((part * factor * gain_ref[pl.ds(source, 1), :]).astype(BF))
        half = near_refs[0].shape[0]
        at = pl.multiple_of(source * channels, channels)
        inside = pl.ds(pl.multiple_of(lax.rem(at, half), channels), channels)
        mine = at // half == core
        line = [own_ref[pl.ds(at, channels), :]]
        for near, far in zip(near_refs, far_refs):
            line.append(jnp.where(mine, near[inside, :], far[inside, :]))
        lines.append(jnp.concatenate(line, axis=1))
    query = jnp.dot(
        jnp.concatenate(normed, axis=1),
        jnp.concatenate(lines, axis=0),
        preferred_element_type=F32,
    )
    for g in range(groups):
        out_ref[g] = (query[:, g * channels : (g + 1) * channels] * scale).astype(BF)


def weight_specs(which, groups, ahead, depth, channels):
    half = depth // 2
    own = pl.BlockSpec((None, depth, channels), lambda *_: (which, 0, 0))
    near = pl.BlockSpec((half, channels), lambda *_: (ahead // half + which, 0))
    far = pl.BlockSpec((half, channels), lambda *_: (which, 0))
    return [own, *[near] * (groups - 1), *[far] * (groups - 1)]


def query_of(place, row, gain, weights, columns, scale):
    own, near, far = weights
    groups = len(row)
    channels = row[0].shape[1]
    depth = own.shape[1]
    block = 256
    return pl.pallas_call(
        functools.partial(query_kernel, scale, groups),
        grid_spec=pltpu.PrefetchScalarGridSpec(
            num_scalar_prefetch=1,
            grid=(columns // block,),
            in_specs=[pl.BlockSpec((block, channels), lambda i, place: (i, 0))] * groups
            + [pl.BlockSpec(gain.shape, lambda i, place: (0, 0))]
            + weight_specs(0, groups, columns, depth, channels),
            out_specs=pl.BlockSpec((groups, block, channels), lambda i, place: (0, i, 0)),
        ),
        out_shape=jax.ShapeDtypeStruct((groups, columns, channels), BF),
        cost_estimate=pl.CostEstimate(flops=2 * 10**9, bytes_accessed=3 * 2**20, transcendentals=0),
        name="query",
    )(place, *row, gain, own, *near, *far)


def attend_kernel(per_group, first, start, block, place_ref, query_hbm, *refs):
    if first:
        blocks_hbm, own_hbm, *refs = refs
    else:
        key_hbm, value_hbm, own_hbm, *refs = refs
    groups, _, channels = query_hbm.shape
    others = groups - 1
    near_hbm, far_hbm, refs = refs[:others], refs[others : 2 * others], refs[2 * others :]
    if first:
        out_ref, key_hbm, value_hbm, query, keys, values, joined, arrive, leave, *refs = refs
        sampled, pairs = refs
    else:
        out_ref, query, keys, values, joined, arrive = refs
    core = place_ref[1]
    width = groups * channels
    half = width // 2
    count = query.shape[1]
    fetches = []

    def fetch(source, target):
        copy = pltpu.make_async_copy(source, target, arrive.at[len(fetches)])
        copy.start()
        fetches.append(copy)
        return copy

    def wait(copies):
        for copy in copies:
            copy.wait()

    def columns_of(g):
        return pl.ds(g * channels, channels)

    if first:
        gathered = [
            fetch(blocks_hbm.at[:, g], sampled.at[:, :, columns_of(g)]) for g in range(groups)
        ]
        paired = [
            [fetch(own_hbm.at[1 + side], pairs.at[0, :, columns_of(side)]) for side in range(2)]
        ]
        for g in range(1, groups):
            paired.append([])
            for side in range(2):
                for half_hbm, at in ((near_hbm[g - 1], core), (far_hbm[g - 1], 1 - core)):
                    lines = pl.ds(pl.multiple_of(at * half, half), half)
                    ahead = half_hbm.shape[0] - 4 * half
                    source = half_hbm.at[pl.ds(ahead + (1 + side) * half, half)]
                    paired[g].append(fetch(source, pairs.at[g, lines, columns_of(side)]))
    asked = fetch(query_hbm.at[:, pl.ds(start, count)], query)
    if not first:
        made = [
            [fetch(key_hbm.at[g], keys.at[g]), fetch(value_hbm.at[g], values.at[g])]
            for g in range(groups)
        ]
    joins = []
    for j in range(groups):
        source = own_hbm.at[3, columns_of(j)]
        joins.append(fetch(source, joined.at[columns_of(0), columns_of(j)]))
    per_half = groups // 2
    for g in range(1, groups):
        for j in range(per_half):
            for half_hbm, at in ((near_hbm[g - 1], core), (far_hbm[g - 1], 1 - core)):
                lanes = pl.ds(pl.multiple_of((at * per_half + j) * channels, channels), channels)
                ahead = half_hbm.shape[0] - half
                source = half_hbm.at[pl.ds(ahead + j * channels, channels)]
                joins.append(fetch(source, joined.at[columns_of(g), lanes]))

    if first:
        stores = []
        wait(gathered)
        points = sampled[...].reshape(keys.shape[1], width)
        for g in range(groups):
            wait(paired[g])
            product = jnp.dot(points, pairs[g], preferred_element_type=F32)
            keys[g] = product[:, :channels].astype(BF)
            values[g] = product[:, channels:].astype(BF)
        for source, target in ((keys, key_hbm), (values, value_hbm)):
            stores.append(pltpu.make_async_copy(source, target, leave.at[len(stores)]))
            stores[-1].start()

    else:
        for copies in made:
            wait(copies)
    asked.wait()
    wait(joins)
    head = lax.broadcasted_iota(jnp.int32, (1, channels), 1) // (channels // per_group)
    zero = jnp.zeros((), BF)
    one = jnp.ones((), BF)

    def one_block(index, carry):
        lines = pl.ds(pl.multiple_of(index * block, block), block)
        attended = []
        for g in range(groups):
            total = jnp.zeros((block, 2 * channels), F32)
            for h in range(per_group):
                key = jnp.where(head == h, keys[g], zero)
                scores = lax.dot_general(
                    query[g, lines, :], key, ROW_BY_ROW, preferred_element_type=F32
                )
                top = jnp.max(scores, axis=-1, keepdims=True)
                probs = jnp.exp2(scores - top).astype(BF)
                value = jnp.where(head == h, values[g], zero)
                ones = jnp.broadcast_to(jnp.where(head == h, one, zero), value.shape)
                both = jnp.concatenate([value, ones], axis=1)
                total = total + jnp.dot(probs, both, preferred_element_type=F32)
            attended.append((total[:, :channels] / total[:, channels:]).astype(BF))
        whole = jnp.concatenate(attended, axis=1)
        projected = jnp.dot(whole, joined[...], preferred_element_type=F32)
        for g in range(groups):
            out_ref[g, lines, :] = projected[:, g * channels : (g + 1) * channels].astype(BF)
        return carry

    lax.fori_loop(0, count // block, one_block, 0)
    if first:
        wait(stores)


def attend_and_project(place, query, source, weights, start, count, block):
    own, near, far = weights
    groups, _, channels = query.shape
    first = len(source) == 1
    width = groups * channels
    points = source[0].size // width
    vmem = pl.BlockSpec(memory_space=pltpu.VMEM)
    anywhere = pl.BlockSpec(memory_space=pl.ANY)
    out_specs, out_shape = vmem, jax.ShapeDtypeStruct((groups, count, channels), BF)
    operands = [query, *source, own, *near, *far]
    pair = (groups, points, channels)
    scratch = [
        pltpu.VMEM((groups, count, channels), BF),
        pltpu.VMEM(pair, BF),
        pltpu.VMEM(pair, BF),
        pltpu.VMEM((width, width), BF),
        pltpu.SemaphoreType.DMA((64,)),
    ]
    if first:
        made = jax.ShapeDtypeStruct(pair, BF)
        out_specs, out_shape = (vmem, anywhere, anywhere), (out_shape, made, made)
        bands, _, share, _ = source[0].shape
        scratch += [
            pltpu.SemaphoreType.DMA((2,)),
            pltpu.VMEM((bands, share, width), BF),
            pltpu.VMEM((groups, width, 2 * channels), BF),
        ]
    return pl.pallas_call(
        functools.partial(attend_kernel, HEADS // groups, first, start, block),
        in_specs=[pl.BlockSpec(memory_space=pltpu.SMEM)] + [anywhere] * len(operands),
        out_specs=out_specs,
        out_shape=out_shape,
        scratch_shapes=scratch,
        cost_estimate=pl.CostEstimate(
            flops=4 * count * points * width, bytes_accessed=4 * 2**20, transcendentals=0
        ),
        name="attend",
    )(place, *operands)


def convolve_kernel(low_ref, normed_ref, high_ref, tokens_ref, taps_ref, out_ref, padded):
    rows, columns, channels = normed_ref.shape
    margin = KER // 2
    pad = 8

    @pl.when(pl.program_id(0) == 0)
    def _():
        padded[:, 0:pad, :] = jnp.zeros((rows + 2 * margin, pad, channels), F32)
        padded[:, pad + columns :, :] = jnp.zeros((rows + 2 * margin, pad, channels), F32)
        padded[0:margin, pad : pad + columns, :] = low_ref[...].astype(F32)
        padded[margin : margin + rows, pad : pad + columns, :] = normed_ref[...].astype(F32)
        padded[margin + rows :, pad : pad + columns, :] = high_ref[...].astype(F32)

    taps = taps_ref[...]
    strip = 16
    span = tokens_ref.shape[1]
    begin = pl.program_id(0) * span

    def one_strip(index, carry):
        inside = pl.multiple_of(index * strip, strip)
        start = pl.multiple_of(begin + inside, strip)
        totals = [tokens_ref[r, pl.ds(inside, strip), :].astype(F32) for r in range(rows)]
        for second in range(KER):
            for line in range(rows + 2 * margin):
                values = padded[line, pl.ds(start + pad - margin + second, strip), :]
                for r in range(rows):
                    first = line - r
                    if 0 <= first < KER:
                        tap = first * KER + second
                        totals[r] = totals[r] + taps[tap : tap + 1, :] * values
        for r in range(rows):
            out_ref[r, pl.ds(inside, strip), :] = totals[r]
        return carry

    lax.fori_loop(0, span // strip, one_strip, 0)


def convolve(low, normed, high, tokens, taps):
    rows, columns, channels = normed.shape
    span = columns // 4
    piece = pl.BlockSpec((rows, span, channels), lambda i: (0, i, 0))
    edge = pl.BlockSpec(low.shape, lambda i: (0, 0, 0))
    return pl.pallas_call(
        convolve_kernel,
        grid=(columns // span,),
        in_specs=[
            edge,
            pl.BlockSpec(normed.shape, lambda i: (0, 0, 0)),
            edge,
            piece,
            pl.BlockSpec(taps.shape, lambda i: (0, 0)),
        ],
        out_specs=piece,
        out_shape=jax.ShapeDtypeStruct(normed.shape, F32),
        scratch_shapes=[pltpu.VMEM((rows + 2 * (KER // 2), columns + 16, channels), F32)],
        cost_estimate=pl.CostEstimate(flops=10**9, bytes_accessed=6 * 2**20, transcendentals=0),
        name="convolve",
    )(low, normed, high, tokens, taps)


def body(
    tokens, corner_row, corner_col, fraction, w_query, w_key, w_value, w_out, conv_kernel, norm_gain
):
    rows, columns, channels = tokens.shape
    groups = lax.axis_size("head")
    bands = lax.axis_size("band")
    width = groups * channels
    points = corner_row.shape[0]
    share = points // bands

    head = lax.axis_index("head")
    core = lax.axis_index("dp")
    place = jnp.stack([head, core])
    moments = local_moments(tokens, groups)
    moments = lax.all_to_all(moments, "head", 0, 0, tiled=True)
    depth = w_query.shape[0]
    out_blocks = [w_out[:, g * channels : (g + 1) * channels] for g in range(groups)]
    own = jnp.stack([w_query, w_key, w_value, jnp.concatenate(out_blocks, axis=0)])
    half = lax.dynamic_slice_in_dim(own, core * (depth // 2), depth // 2, 1)
    half = half.reshape(2 * depth, channels)

    def to_all_heads(blocks):
        arrived = {}
        for distance in (2, 1, 3):
            ring = [(i, (i + distance) % groups) for i in range(groups)]
            arrived[distance] = lax.ppermute(blocks[distance], "head", ring)
        return [arrived[distance] for distance in range(1, groups)]

    token_rows = [
        lax.dynamic_index_in_dim(tokens, (head + distance) % groups, 0, keepdims=False)
        for distance in range(groups)
    ]
    bulk = [jnp.concatenate([rows_out, half], axis=0) for rows_out in token_rows]
    near = to_all_heads(bulk)
    token_rows = [token_rows[0], *near]
    far = [lax.ppermute(a[columns:], "dp", [(0, 1), (1, 0)]) for a in near]
    weights = (own, near, far)
    gain = norm_gain.reshape(groups, channels)

    table, weight = tables(
        lax.axis_index("band").reshape(1), corner_row, corner_col, fraction, columns, rows
    )
    normed, low, high, partial = normalize_and_sample(place, gain, tokens, moments, table, weight)

    parts = lax.all_to_all(partial.reshape(bands, share, channels), "band", 0, 0, tiled=True)
    forward = [(i, i + 1) for i in range(bands - 1)]
    backward = [(target, source) for source, target in forward]
    low = lax.ppermute(low, "band", forward)
    high = lax.ppermute(high, "band", backward)
    piece = jnp.sum(parts.astype(F32), axis=0).astype(BF)
    copies = jnp.broadcast_to(piece, (bands * groups, *piece.shape))
    blocks = lax.all_to_all(copies, ("band", "head"), 0, 0, tiled=True)
    blocks = blocks.reshape(bands, groups, share, channels)

    size = width // HEADS
    scale = 1.4426950408889634 / size**0.5
    query = query_of(place, token_rows, gain, weights, columns, scale)
    base = convolve(low, normed, high, tokens, conv_kernel)
    half_way = columns // 2
    chunks = ((0, half_way, half_way // 2), (half_way, half_way, half_way // 2))
    returned = []
    source = (blocks,)
    for chunk, (start, count, block) in enumerate(chunks):
        projected = attend_and_project(place, query, source, weights, start, count, block)
        if chunk == 0:
            projected, *source = projected
        returned.append(lax.all_to_all(projected, "head", 0, 0, tiled=True))
    projected = jnp.concatenate(returned, axis=1)
    return (base + projected.astype(F32)).astype(BF)


def solution(mesh):
    return jax.shard_map(
        body,
        mesh=mesh,
        in_specs=(
            P(("dp", "band"), None, "head"),
            P("dp"),
            P("dp"),
            P(None, "dp"),
            P(None, "head"),
            P(None, "head"),
            P(None, "head"),
            P("head", None),
            P(None, "head"),
            P(),
        ),
        out_specs=P(("dp", "band"), None, "head"),
        check_vma=False,
    )
```

```python
import functools

import jax
import jax.numpy as jnp
from jax import lax
from jax.experimental import pallas as pl
from jax.experimental.pallas import tpu as pltpu
from jax.sharding import PartitionSpec as P


HEADS = 16
KER = 5
EPS = 1e-05
F32 = jnp.float32
BF = jnp.bfloat16
ROW_BY_ROW = (((1,), (1,)), ((), ()))
COLUMN_BY_COLUMN = (((0,), (0,)), ((), ()))


def split_in_three(x):
    high = x.astype(BF)
    rest = x - high.astype(F32)
    middle = rest.astype(BF)
    return high, middle, (rest - middle.astype(F32)).astype(BF)


def moments_kernel(
    place_ref, tokens_ref, query_ref, key_ref, value_ref, out_weight_ref, moments_ref, own_ref, *refs
):
    *bulk_hbm, half, leave = refs
    rows, columns, channels = tokens_ref.shape
    depth = query_ref.shape[0]
    for index, ref in enumerate((query_ref, key_ref, value_ref)):
        own_ref[index] = ref[...]
    for g in range(rows):
        at = slice(g * channels, (g + 1) * channels)
        own_ref[3, at, :] = out_weight_ref[:, at]
    cut = depth // 2
    lines = pl.ds(pl.multiple_of(place_ref[1] * cut, cut), cut)
    for index in range(4):
        half[index * cut : (index + 1) * cut, :] = own_ref[index, lines, :]
    stores = []
    for distance, target in enumerate(bulk_hbm, 1):
        row = lax.rem(place_ref[0] + distance, rows)
        for source, start in ((tokens_ref.at[row], 0), (half, columns)):
            place = target.at[pl.ds(start, source.shape[0])]
            stores.append(pltpu.make_async_copy(source, place, leave.at[len(stores)]))
            stores[-1].start()
    side = lax.broadcasted_iota(jnp.int32, (8, 2 * channels), 1) // channels
    pick = jnp.where(side == lax.broadcasted_iota(jnp.int32, (8, 2 * channels), 0), 1.0, 0.0)
    pick = pick.astype(BF)
    average = jnp.full((channels, channels), 1.0 / channels, BF)
    for row in range(rows):
        block = tokens_ref[row]
        center = jnp.dot(block, average, preferred_element_type=F32)
        square = jnp.square(block.astype(F32) - center).astype(BF)
        both = jnp.concatenate([block, square], axis=1)
        facts = lax.dot_general(pick, both, ROW_BY_ROW, preferred_element_type=F32)
        at = pl.ds(row * columns, columns)
        for copy in range(moments_ref.shape[0]):
            moments_ref[copy, :, at] = facts[0:2]
    for store in stores:
        store.wait()


def moments_and_bulk(place, tokens, w_query, w_key, w_value, w_out, copies):
    rows, columns, channels = tokens.shape
    depth = w_query.shape[0]
    vmem = pl.BlockSpec(memory_space=pltpu.VMEM)
    anywhere = pl.BlockSpec(memory_space=pl.ANY)
    bulk = jax.ShapeDtypeStruct((columns + 2 * depth, channels), BF)
    moments, own, *bulk = pl.pallas_call(
        moments_kernel,
        in_specs=[pl.BlockSpec(memory_space=pltpu.SMEM)] + [vmem] * 5,
        out_specs=(vmem, vmem, *[anywhere] * (copies - 1)),
        out_shape=(
            jax.ShapeDtypeStruct((copies, 2, rows * columns), F32),
            jax.ShapeDtypeStruct((4, depth, channels), BF),
            *[bulk] * (copies - 1),
        ),
        scratch_shapes=[
            pltpu.VMEM((2 * depth, channels), BF),
            pltpu.SemaphoreType.DMA((2 * copies,)),
        ],
        cost_estimate=pl.CostEstimate(flops=10**9, bytes_accessed=2**20, transcendentals=0),
        name="moments",
    )(place, tokens, w_query, w_key, w_value, w_out)
    return moments, own, bulk


def make_tables(band, row_ref, column_ref, fraction_ref, table_ref, weight_ref):
    _, columns = table_ref.shape
    rows = weight_ref.shape[1] // 128
    lines = row_ref[...]
    start = band * rows
    column = column_ref[...]
    vertical = fraction_ref[0:1, :]
    horizontal = fraction_ref[1:2, :]
    top = (1.0 - vertical).astype(BF).astype(F32)
    bottom = vertical.astype(BF).astype(F32)
    coarse = (column // 8) * 8
    facts = [
        coarse.astype(F32),
        (column - coarse).astype(F32),
        (1.0 - horizontal).astype(BF).astype(F32),
        horizontal.astype(BF).astype(F32),
    ]
    for r in range(rows):
        here = jnp.where(lines == start + r, top, 0.0)
        facts.append(here + jnp.where(lines + 1 == start + r, bottom, 0.0))
    facts += [jnp.zeros_like(facts[0])] * (16 - len(facts))
    facts = jnp.concatenate(facts, axis=0).astype(BF)
    kinds = 3 + rows
    fact = lax.broadcasted_iota(jnp.int32, (16, kinds * 128), 0)
    kind = lax.broadcasted_iota(jnp.int32, (16, kinds * 128), 1) // 128
    pick = (jnp.maximum(fact - 1, 0) == kind) & (fact < kinds + 1)
    spread = lax.dot_general(
        facts,
        jnp.where(pick, 1.0, 0.0).astype(BF),
        COLUMN_BY_COLUMN,
        preferred_element_type=F32,
    )
    weight_ref[...] = spread[:, 3 * 128 :].astype(BF)
    middle = spread[:, :128]
    left, right = spread[:, 128:256], spread[:, 256:384]
    lane = lax.broadcasted_iota(jnp.int32, (1, 128), 1).astype(F32)
    for block in range(columns // 128):
        offset = lane + float(block * 128) - middle
        values = jnp.where(offset == 0.0, left, jnp.where(offset == 1.0, right, 0.0))
        table_ref[:, block * 128 : (block + 1) * 128] = values.astype(BF)


def normalize_sample_kernel(
    place_ref,
    gain_ref,
    row_ref,
    column_ref,
    fraction_ref,
    tokens_hbm,
    moments_hbm,
    normed_hbm,
    low_hbm,
    high_hbm,
    sampled_ref,
    tokens,
    moments,
    table,
    weights,
    normed,
    planes,
    arrive,
    leave,
):
    fetches = []
    for index, (source, target) in enumerate(
        ((moments_hbm, moments), (tokens_hbm, tokens))
    ):
        fetches.append(pltpu.make_async_copy(source, target, arrive.at[index]))
        fetches[-1].start()
    rows, columns, channels = tokens.shape
    devices = moments.shape[0]
    make_tables(place_ref[2], row_ref, column_ref, fraction_ref, table, weights)
    fetches[0].wait()
    sums = [moments[d, 0:1, :] for d in range(devices)]
    width = channels * devices
    center = functools.reduce(jnp.add, sums) * (1.0 / width)
    spread = functools.reduce(jnp.add, [moments[d, 1:2, :] for d in range(devices)])
    for d in range(devices):
        spread = spread + channels * jnp.square(sums[d] * (1.0 / channels) - center)
    factor = lax.rsqrt(spread * (1.0 / width) + EPS)
    pieces = [*split_in_three(center), *split_in_three(factor)]
    pieces += [jnp.zeros_like(pieces[0])] * 10
    stacked = jnp.concatenate([p.astype(F32) for p in pieces], axis=0).astype(BF)
    piece = lax.broadcasted_iota(jnp.int32, (16, 2 * channels), 0)
    lane = lax.broadcasted_iota(jnp.int32, (16, 2 * channels), 1)
    pick = jnp.where((piece < 6) & (piece // 3 == lane // channels), 1.0, 0.0).astype(BF)
    gain = gain_ref[pl.ds(place_ref[0], 1), :]
    margin = KER // 2
    fetches[1].wait()
    stores = []

    def send(source, target):
        stores.append(pltpu.make_async_copy(source, target, leave.at[len(stores)]))
        stores[-1].start()

    for row in range(rows):
        part = stacked[:, row * columns : (row + 1) * columns]
        spreadout = lax.dot_general(part, pick, COLUMN_BY_COLUMN, preferred_element_type=F32)
        values = tokens[row].astype(F32) - spreadout[:, :channels]
        values = (values * spreadout[:, channels:] * gain).astype(BF)
        normed[row] = values
        planes[:, row * channels : (row + 1) * channels] = values
    send(normed, normed_hbm)
    send(normed.at[pl.ds(rows - margin, margin)], low_hbm)
    send(normed.at[pl.ds(0, margin)], high_hbm)
    inner = jnp.dot(table[...], planes[...], preferred_element_type=F32)
    total = None
    for row in range(rows):
        at = slice(row * channels, (row + 1) * channels)
        part = weights[:, at].astype(F32) * inner[:, at]
        total = part if total is None else total + part
    sampled_ref[...] = total.astype(BF)
    for store in stores:
        store.wait()


def normalize_and_sample(place, gain, corner_row, corner_col, fraction, tokens, moments):
    rows, columns, channels = tokens.shape
    points = corner_row.shape[0]
    vmem = pl.BlockSpec(memory_space=pltpu.VMEM)
    anywhere = pl.BlockSpec(memory_space=pl.ANY)
    edge = jax.ShapeDtypeStruct((KER // 2, columns, channels), BF)
    return pl.pallas_call(
        normalize_sample_kernel,
        in_specs=[pl.BlockSpec(memory_space=pltpu.SMEM)] + [vmem] * 4 + [anywhere] * 2,
        out_specs=(anywhere, anywhere, anywhere, vmem),
        out_shape=(
            jax.ShapeDtypeStruct(tokens.shape, BF),
            edge,
            edge,
            jax.ShapeDtypeStruct((points, channels), BF),
        ),
        scratch_shapes=[
            pltpu.VMEM(tokens.shape, BF),
            pltpu.VMEM(moments.shape, F32),
            pltpu.VMEM((points, columns), BF),
            pltpu.VMEM((points, rows * channels), BF),
            pltpu.VMEM(tokens.shape, BF),
            pltpu.VMEM((columns, rows * channels), BF),
            pltpu.SemaphoreType.DMA((2,)),
            pltpu.SemaphoreType.DMA((3,)),
        ],
        cost_estimate=pl.CostEstimate(flops=2 * 10**9, bytes_accessed=6 * 2**20, transcendentals=0),
        name="normalize_sample",
    )(
        place,
        gain,
        corner_row.reshape(1, points),
        corner_col.reshape(1, points),
        fraction,
        tokens,
        moments,
    )


def query_kernel(scale, groups, place_ref, *refs):
    row_refs, refs = refs[:groups], refs[groups:]
    gain_ref, own_ref, *rest = refs
    near_refs, far_refs, (out_ref,) = rest[: groups - 1], rest[groups - 1 : -1], rest[-1:]
    channels = row_refs[0].shape[1]
    width = groups * channels
    place, core = place_ref[0], place_ref[1]
    parts = [ref[...].astype(F32) for ref in row_refs]
    center = sum(jnp.sum(p, axis=1, keepdims=True) for p in parts) * (1.0 / width)
    parts = [p - center for p in parts]
    spread = sum(jnp.sum(jnp.square(p), axis=1, keepdims=True) for p in parts) * (1.0 / width)
    factor = lax.rsqrt(spread + EPS)
    normed, lines = [], []
    for distance, part in enumerate(parts):
        source = lax.rem(place + (groups - distance), groups)
        normed.append((part * factor * gain_ref[pl.ds(source, 1), :]).astype(BF))
        half = near_refs[0].shape[0]
        at = pl.multiple_of(source * channels, channels)
        inside = pl.ds(pl.multiple_of(lax.rem(at, half), channels), channels)
        mine = at // half == core
        line = [own_ref[pl.ds(at, channels), :]]
        for near, far in zip(near_refs, far_refs):
            line.append(jnp.where(mine, near[inside, :], far[inside, :]))
        lines.append(jnp.concatenate(line, axis=1))
    query = jnp.dot(
        jnp.concatenate(normed, axis=1),
        jnp.concatenate(lines, axis=0),
        preferred_element_type=F32,
    )
    for g in range(groups):
        out_ref[g] = (query[:, g * channels : (g + 1) * channels] * scale).astype(BF)


def weight_specs(which, groups, ahead, depth, channels):
    half = depth // 2
    own = pl.BlockSpec((None, depth, channels), lambda *_: (which, 0, 0))
    near = pl.BlockSpec((half, channels), lambda *_: (ahead // half + which, 0))
    far = pl.BlockSpec((half, channels), lambda *_: (which, 0))
    return [own, *[near] * (groups - 1), *[far] * (groups - 1)]


def query_of(place, row, gain, weights, columns, scale):
    own, near, far = weights
    groups = len(row)
    channels = own.shape[2]
    depth = own.shape[1]
    block = 256
    return pl.pallas_call(
        functools.partial(query_kernel, scale, groups),
        grid_spec=pltpu.PrefetchScalarGridSpec(
            num_scalar_prefetch=1,
            grid=(columns // block,),
            in_specs=[pl.BlockSpec((None, block, channels), lambda i, place: (place[0], i, 0))]
            + [pl.BlockSpec((block, channels), lambda i, place: (i, 0))] * (groups - 1)
            + [pl.BlockSpec(gain.shape, lambda i, place: (0, 0))]
            + weight_specs(0, groups, columns, depth, channels),
            out_specs=pl.BlockSpec((groups, block, channels), lambda i, place: (0, i, 0)),
        ),
        out_shape=jax.ShapeDtypeStruct((groups, columns, channels), BF),
        cost_estimate=pl.CostEstimate(flops=2 * 10**9, bytes_accessed=3 * 2**20, transcendentals=0),
        name="query",
    )(place, *row, gain, own, *near, *far)


def attend_kernel(per_group, first, start, block, place_ref, query_hbm, *refs):
    if first:
        blocks_hbm, own_hbm, *refs = refs
    else:
        key_hbm, value_hbm, own_hbm, *refs = refs
    groups, _, channels = query_hbm.shape
    others = groups - 1
    near_hbm, far_hbm, refs = refs[:others], refs[others : 2 * others], refs[2 * others :]
    if first:
        out_ref, key_hbm, value_hbm, query, keys, values, joined, arrive, leave, *refs = refs
        sampled, pairs = refs
    else:
        out_ref, query, keys, values, joined, arrive = refs
    core = place_ref[1]
    width = groups * channels
    half = width // 2
    count = query.shape[1]
    fetches = []

    def fetch(source, target):
        copy = pltpu.make_async_copy(source, target, arrive.at[len(fetches)])
        copy.start()
        fetches.append(copy)
        return copy

    def wait(copies):
        for copy in copies:
            copy.wait()

    def columns_of(g):
        return pl.ds(g * channels, channels)

    if first:
        gathered = [
            fetch(blocks_hbm.at[:, g], sampled.at[:, :, columns_of(g)]) for g in range(groups)
        ]
        paired = [
            [fetch(own_hbm.at[1 + side], pairs.at[0, :, columns_of(side)]) for side in range(2)]
        ]
        for g in range(1, groups):
            paired.append([])
            for side in range(2):
                for half_hbm, at in ((near_hbm[g - 1], core), (far_hbm[g - 1], 1 - core)):
                    lines = pl.ds(pl.multiple_of(at * half, half), half)
                    ahead = half_hbm.shape[0] - 4 * half
                    source = half_hbm.at[pl.ds(ahead + (1 + side) * half, half)]
                    paired[g].append(fetch(source, pairs.at[g, lines, columns_of(side)]))
    asked = fetch(query_hbm.at[:, pl.ds(start, count)], query)
    if not first:
        made = [
            [fetch(key_hbm.at[g], keys.at[g]), fetch(value_hbm.at[g], values.at[g])]
            for g in range(groups)
        ]
    joins = []
    for j in range(groups):
        source = own_hbm.at[3, columns_of(j)]
        joins.append(fetch(source, joined.at[columns_of(0), columns_of(j)]))
    per_half = groups // 2
    for g in range(1, groups):
        for j in range(per_half):
            for half_hbm, at in ((near_hbm[g - 1], core), (far_hbm[g - 1], 1 - core)):
                lanes = pl.ds(pl.multiple_of((at * per_half + j) * channels, channels), channels)
                ahead = half_hbm.shape[0] - half
                source = half_hbm.at[pl.ds(ahead + j * channels, channels)]
                joins.append(fetch(source, joined.at[columns_of(g), lanes]))

    if first:
        stores = []
        wait(gathered)
        points = sampled[...].reshape(keys.shape[1], width)
        for g in range(groups):
            wait(paired[g])
            product = jnp.dot(points, pairs[g], preferred_element_type=F32)
            keys[g] = product[:, :channels].astype(BF)
            values[g] = product[:, channels:].astype(BF)
        for source, target in ((keys, key_hbm), (values, value_hbm)):
            stores.append(pltpu.make_async_copy(source, target, leave.at[len(stores)]))
            stores[-1].start()

    else:
        for copies in made:
            wait(copies)
    asked.wait()
    wait(joins)
    head = lax.broadcasted_iota(jnp.int32, (1, channels), 1) // (channels // per_group)
    zero = jnp.zeros((), BF)
    one = jnp.ones((), BF)

    def one_block(index, carry):
        lines = pl.ds(pl.multiple_of(index * block, block), block)
        attended = []
        for g in range(groups):
            total = jnp.zeros((block, 2 * channels), F32)
            for h in range(per_group):
                key = jnp.where(head == h, keys[g], zero)
                scores = lax.dot_general(
                    query[g, lines, :], key, ROW_BY_ROW, preferred_element_type=F32
                )
                top = jnp.max(scores, axis=-1, keepdims=True)
                probs = jnp.exp2(scores - top).astype(BF)
                value = jnp.where(head == h, values[g], zero)
                ones = jnp.broadcast_to(jnp.where(head == h, one, zero), value.shape)
                both = jnp.concatenate([value, ones], axis=1)
                total = total + jnp.dot(probs, both, preferred_element_type=F32)
            attended.append((total[:, :channels] / total[:, channels:]).astype(BF))
        whole = jnp.concatenate(attended, axis=1)
        projected = jnp.dot(whole, joined[...], preferred_element_type=F32)
        for g in range(groups):
            out_ref[g, lines, :] = projected[:, g * channels : (g + 1) * channels].astype(BF)
        return carry

    lax.fori_loop(0, count // block, one_block, 0)
    if first:
        wait(stores)


def attend_and_project(place, query, source, weights, start, count, block):
    own, near, far = weights
    groups, _, channels = query.shape
    first = len(source) == 1
    width = groups * channels
    points = source[0].size // width
    vmem = pl.BlockSpec(memory_space=pltpu.VMEM)
    anywhere = pl.BlockSpec(memory_space=pl.ANY)
    out_specs, out_shape = vmem, jax.ShapeDtypeStruct((groups, count, channels), BF)
    operands = [query, *source, own, *near, *far]
    pair = (groups, points, channels)
    scratch = [
        pltpu.VMEM((groups, count, channels), BF),
        pltpu.VMEM(pair, BF),
        pltpu.VMEM(pair, BF),
        pltpu.VMEM((width, width), BF),
        pltpu.SemaphoreType.DMA((64,)),
    ]
    if first:
        made = jax.ShapeDtypeStruct(pair, BF)
        out_specs, out_shape = (vmem, anywhere, anywhere), (out_shape, made, made)
        bands, _, share, _ = source[0].shape
        scratch += [
            pltpu.SemaphoreType.DMA((2,)),
            pltpu.VMEM((bands, share, width), BF),
            pltpu.VMEM((groups, width, 2 * channels), BF),
        ]
    return pl.pallas_call(
        functools.partial(attend_kernel, HEADS // groups, first, start, block),
        in_specs=[pl.BlockSpec(memory_space=pltpu.SMEM)] + [anywhere] * len(operands),
        out_specs=out_specs,
        out_shape=out_shape,
        scratch_shapes=scratch,
        cost_estimate=pl.CostEstimate(
            flops=4 * count * points * width, bytes_accessed=4 * 2**20, transcendentals=0
        ),
        name="attend",
    )(place, *operands)


def convolve_kernel(
    low_ref, normed_ref, high_ref, tokens_ref, added_ref, taps_ref, mixed_ref, base_ref, padded
):
    rows, columns, channels = normed_ref.shape
    margin = KER // 2
    pad = 8
    step = pl.program_id(0)
    finished = pl.num_programs(0) // 2

    @pl.when(step == 0)
    def _():
        padded[:, 0:pad, :] = jnp.zeros((rows + 2 * margin, pad, channels), F32)
        padded[:, pad + columns :, :] = jnp.zeros((rows + 2 * margin, pad, channels), F32)
        padded[0:margin, pad : pad + columns, :] = low_ref[...].astype(F32)
        padded[margin : margin + rows, pad : pad + columns, :] = normed_ref[...].astype(F32)
        padded[margin + rows :, pad : pad + columns, :] = high_ref[...].astype(F32)

    taps = taps_ref[...]
    strip = 16
    span = tokens_ref.shape[1]
    begin = step * span

    def convolve_into(out_ref, added):
        def one_strip(index, carry):
            inside = pl.multiple_of(index * strip, strip)
            at = pl.ds(inside, strip)
            start = pl.multiple_of(begin + inside, strip)
            totals = [tokens_ref[r, at, :].astype(F32) for r in range(rows)]
            if added:
                totals = [t + added_ref[r, at, :].astype(F32) for r, t in enumerate(totals)]
            for second in range(KER):
                for line in range(rows + 2 * margin):
                    values = padded[line, pl.ds(start + pad - margin + second, strip), :]
                    for r in range(rows):
                        first = line - r
                        if 0 <= first < KER:
                            tap = first * KER + second
                            totals[r] = totals[r] + taps[tap : tap + 1, :] * values
            for r in range(rows):
                out_ref[r, at, :] = totals[r].astype(out_ref.dtype)
            return carry

        lax.fori_loop(0, span // strip, one_strip, 0)

    @pl.when(step < finished)
    def _():
        convolve_into(mixed_ref, True)

    @pl.when(step >= finished)
    def _():
        convolve_into(base_ref, False)


def convolve(low, normed, high, tokens, added, taps):
    rows, columns, channels = normed.shape
    steps = 4
    span = columns // steps
    last = steps // 2 - 1
    whole = pl.BlockSpec(normed.shape, lambda i: (0, 0, 0))
    piece = pl.BlockSpec((rows, span, channels), lambda i: (0, i, 0))
    front = pl.BlockSpec((rows, span, channels), lambda i: (0, jnp.minimum(i, last), 0))
    back = pl.BlockSpec((rows, span, channels), lambda i: (0, jnp.maximum(i - last - 1, 0), 0))
    edge = pl.BlockSpec(low.shape, lambda i: (0, 0, 0))
    return pl.pallas_call(
        convolve_kernel,
        grid=(steps,),
        in_specs=[edge, whole, edge, piece, front, pl.BlockSpec(taps.shape, lambda i: (0, 0))],
        out_specs=(front, back),
        out_shape=(
            jax.ShapeDtypeStruct(normed.shape, BF),
            jax.ShapeDtypeStruct((rows, columns // 2, channels), F32),
        ),
        scratch_shapes=[pltpu.VMEM((rows + 2 * (KER // 2), columns + 16, channels), F32)],
        cost_estimate=pl.CostEstimate(flops=10**9, bytes_accessed=6 * 2**20, transcendentals=0),
        name="convolve",
    )(low, normed, high, tokens, added, taps)


def body(
    tokens, corner_row, corner_col, fraction, w_query, w_key, w_value, w_out, conv_kernel, norm_gain
):
    _, columns, channels = tokens.shape
    groups = lax.axis_size("head")
    bands = lax.axis_size("band")
    width = groups * channels
    points = corner_row.shape[0]
    share = points // bands

    head = lax.axis_index("head")
    core = lax.axis_index("dp")
    place = jnp.stack([head, core, lax.axis_index("band")])
    moments, own, bulk = moments_and_bulk(
        place, tokens, w_query, w_key, w_value, w_out, groups
    )
    moments = lax.all_to_all(moments, "head", 0, 0, tiled=True)

    def to_all_heads(blocks):
        arrived = {}
        for distance in (2, 1, 3):
            ring = [(i, (i + distance) % groups) for i in range(groups)]
            arrived[distance] = lax.ppermute(blocks[distance], "head", ring)
        return [arrived[distance] for distance in range(1, groups)]

    near = to_all_heads([None, *bulk])
    token_rows = [tokens, *near]
    far = [lax.ppermute(a[columns:], "dp", [(0, 1), (1, 0)]) for a in near]
    weights = (own, near, far)
    gain = norm_gain.reshape(groups, channels)

    normed, low, high, partial = normalize_and_sample(
        place, gain, corner_row, corner_col, fraction, tokens, moments
    )

    parts = lax.all_to_all(partial.reshape(bands, share, channels), "band", 0, 0, tiled=True)
    forward = [(i, i + 1) for i in range(bands - 1)]
    backward = [(target, source) for source, target in forward]
    low = lax.ppermute(low, "band", forward)
    high = lax.ppermute(high, "band", backward)
    piece = jnp.sum(parts.astype(F32), axis=0).astype(BF)
    copies = jnp.broadcast_to(piece, (bands * groups, *piece.shape))
    blocks = lax.all_to_all(copies, ("band", "head"), 0, 0, tiled=True)
    blocks = blocks.reshape(bands, groups, share, channels)

    size = width // HEADS
    scale = 1.4426950408889634 / size**0.5
    query = query_of(place, token_rows, gain, weights, columns, scale)
    half_way = columns // 2
    chunks = ((0, half_way, half_way // 2), (half_way, half_way, half_way // 2))
    returned = []
    source = (blocks,)
    for chunk, (start, count, block) in enumerate(chunks):
        projected = attend_and_project(place, query, source, weights, start, count, block)
        if chunk == 0:
            projected, *source = projected
        returned.append(lax.all_to_all(projected, "head", 0, 0, tiled=True))
    mixed, base = convolve(low, normed, high, tokens, returned[0], conv_kernel)
    rest = (base + returned[1].astype(F32)).astype(BF)
    return lax.dynamic_update_slice_in_dim(mixed, rest, half_way, 1)


def solution(mesh):
    return jax.shard_map(
        body,
        mesh=mesh,
        in_specs=(
            P(("dp", "band"), None, "head"),
            P("dp"),
            P("dp"),
            P(None, "dp"),
            P(None, "head"),
            P(None, "head"),
            P(None, "head"),
            P("head", None),
            P(None, "head"),
            P(),
        ),
        out_specs=P(("dp", "band"), None, "head"),
        check_vma=False,
    )
```

```python
import functools

import jax
import jax.numpy as jnp
from jax import lax
from jax.experimental import pallas as pl
from jax.experimental.pallas import tpu as pltpu
from jax.sharding import PartitionSpec as P


HEADS = 16
KER = 5
EPS = 1e-05
F32 = jnp.float32
BF = jnp.bfloat16
ROW_BY_ROW = (((1,), (1,)), ((), ()))
COLUMN_BY_COLUMN = (((0,), (0,)), ((), ()))


def split_in_three(x):
    high = x.astype(BF)
    rest = x - high.astype(F32)
    middle = rest.astype(BF)
    return high, middle, (rest - middle.astype(F32)).astype(BF)


def moments_kernel(
    tokens_hbm, query_hbm, key_hbm, value_hbm, out_weight_hbm, moments_ref, own_hbm, *refs
):
    *bulk_hbm, tokens_ref, own, half, arrive, leave = refs
    rows, columns, channels = tokens_ref.shape
    depth = query_hbm.shape[0]
    fetches = []

    def fetch(source, target):
        fetches.append(pltpu.make_async_copy(source, target, arrive.at[len(fetches)]))
        fetches[-1].start()

    for row in range(rows):
        fetch(tokens_hbm.at[row], tokens_ref.at[row])
    for index, source in enumerate((query_hbm, key_hbm, value_hbm)):
        fetch(source, own.at[index])
    for g in range(rows):
        at = pl.ds(g * channels, channels)
        fetch(out_weight_hbm.at[:, at], own.at[3, at])
    for waited in fetches:
        waited.wait()
    stores = []

    def send(source, target):
        stores.append(pltpu.make_async_copy(source, target, leave.at[len(stores)]))
        stores[-1].start()

    send(own, own_hbm)
    for distance, target in enumerate(bulk_hbm, 1):
        row = lax.rem(lax.axis_index("head") + distance, rows)
        send(tokens_ref.at[row], target.at[pl.ds(0, columns)])
    cut = depth // 2
    lines = pl.ds(pl.multiple_of(lax.axis_index("dp") * cut, cut), cut)
    for index in range(4):
        half[index * cut : (index + 1) * cut, :] = own[index, lines, :]
    for target in bulk_hbm:
        send(half, target.at[pl.ds(columns, 2 * depth)])
    side = lax.broadcasted_iota(jnp.int32, (8, 2 * channels), 1) // channels
    pick = jnp.where(side == lax.broadcasted_iota(jnp.int32, (8, 2 * channels), 0), 1.0, 0.0)
    pick = pick.astype(BF)
    average = jnp.full((channels, channels), 1.0 / channels, BF)
    for row in range(rows):
        block = tokens_ref[row]
        center = jnp.dot(block, average, preferred_element_type=F32)
        square = jnp.square(block.astype(F32) - center).astype(BF)
        both = jnp.concatenate([block, square], axis=1)
        facts = lax.dot_general(pick, both, ROW_BY_ROW, preferred_element_type=F32)
        at = pl.ds(row * columns, columns)
        for copy in range(moments_ref.shape[0]):
            moments_ref[copy, :, at] = facts[0:2]
    for store in stores:
        store.wait()


def moments_and_bulk(tokens, w_query, w_key, w_value, w_out, copies):
    rows, columns, channels = tokens.shape
    depth = w_query.shape[0]
    vmem = pl.BlockSpec(memory_space=pltpu.VMEM)
    anywhere = pl.BlockSpec(memory_space=pl.ANY)
    bulk = jax.ShapeDtypeStruct((columns + 2 * depth, channels), BF)
    moments, own, *bulk = pl.pallas_call(
        moments_kernel,
        in_specs=[anywhere] * 5,
        out_specs=(vmem, anywhere, *[anywhere] * (copies - 1)),
        out_shape=(
            jax.ShapeDtypeStruct((copies, 2, rows * columns), F32),
            jax.ShapeDtypeStruct((4, depth, channels), BF),
            *[bulk] * (copies - 1),
        ),
        scratch_shapes=[
            pltpu.VMEM(tokens.shape, BF),
            pltpu.VMEM((4, depth, channels), BF),
            pltpu.VMEM((2 * depth, channels), BF),
            pltpu.SemaphoreType.DMA((2 * rows + 3,)),
            pltpu.SemaphoreType.DMA((2 * copies - 1,)),
        ],
        cost_estimate=pl.CostEstimate(flops=10**9, bytes_accessed=2**20, transcendentals=0),
        name="moments",
    )(tokens, w_query, w_key, w_value, w_out)
    return moments, own, bulk


def make_tables(band, row_ref, column_ref, fraction_ref, table_ref, weight_ref):
    _, columns = table_ref.shape
    rows = weight_ref.shape[1] // 128
    lines = row_ref[...]
    start = band * rows
    column = column_ref[...]
    vertical = fraction_ref[0:1, :]
    horizontal = fraction_ref[1:2, :]
    top = (1.0 - vertical).astype(BF).astype(F32)
    bottom = vertical.astype(BF).astype(F32)
    coarse = (column // 8) * 8
    facts = [
        coarse.astype(F32),
        (column - coarse).astype(F32),
        (1.0 - horizontal).astype(BF).astype(F32),
        horizontal.astype(BF).astype(F32),
    ]
    for r in range(rows):
        here = jnp.where(lines == start + r, top, 0.0)
        facts.append(here + jnp.where(lines + 1 == start + r, bottom, 0.0))
    facts += [jnp.zeros_like(facts[0])] * (16 - len(facts))
    facts = jnp.concatenate(facts, axis=0).astype(BF)
    kinds = 3 + rows
    fact = lax.broadcasted_iota(jnp.int32, (16, kinds * 128), 0)
    kind = lax.broadcasted_iota(jnp.int32, (16, kinds * 128), 1) // 128
    pick = (jnp.maximum(fact - 1, 0) == kind) & (fact < kinds + 1)
    spread = lax.dot_general(
        facts,
        jnp.where(pick, 1.0, 0.0).astype(BF),
        COLUMN_BY_COLUMN,
        preferred_element_type=F32,
    )
    weight_ref[...] = spread[:, 3 * 128 :].astype(BF)
    middle = spread[:, :128]
    left, right = spread[:, 128:256], spread[:, 256:384]
    lane = lax.broadcasted_iota(jnp.int32, (1, 128), 1).astype(F32)
    for block in range(columns // 128):
        offset = lane + float(block * 128) - middle
        values = jnp.where(offset == 0.0, left, jnp.where(offset == 1.0, right, 0.0))
        table_ref[:, block * 128 : (block + 1) * 128] = values.astype(BF)


def normalize_sample_kernel(
    gain_ref,
    row_ref,
    column_ref,
    fraction_ref,
    tokens_hbm,
    moments_hbm,
    normed_hbm,
    low_hbm,
    high_hbm,
    sampled_ref,
    tokens,
    moments,
    table,
    weights,
    normed,
    planes,
    arrive,
    leave,
):
    fetches = []
    for index, (source, target) in enumerate(
        ((moments_hbm, moments), (tokens_hbm, tokens))
    ):
        fetches.append(pltpu.make_async_copy(source, target, arrive.at[index]))
        fetches[-1].start()
    rows, columns, channels = tokens.shape
    devices = moments.shape[0]
    make_tables(lax.axis_index("band"), row_ref, column_ref, fraction_ref, table, weights)
    fetches[0].wait()
    sums = [moments[d, 0:1, :] for d in range(devices)]
    width = channels * devices
    center = functools.reduce(jnp.add, sums) * (1.0 / width)
    spread = functools.reduce(jnp.add, [moments[d, 1:2, :] for d in range(devices)])
    for d in range(devices):
        spread = spread + channels * jnp.square(sums[d] * (1.0 / channels) - center)
    factor = lax.rsqrt(spread * (1.0 / width) + EPS)
    pieces = [*split_in_three(center), *split_in_three(factor)]
    pieces += [jnp.zeros_like(pieces[0])] * 10
    stacked = jnp.concatenate([p.astype(F32) for p in pieces], axis=0).astype(BF)
    piece = lax.broadcasted_iota(jnp.int32, (16, 2 * channels), 0)
    lane = lax.broadcasted_iota(jnp.int32, (16, 2 * channels), 1)
    pick = jnp.where((piece < 6) & (piece // 3 == lane // channels), 1.0, 0.0).astype(BF)
    gain = gain_ref[pl.ds(lax.axis_index("head"), 1), :]
    margin = KER // 2
    fetches[1].wait()
    stores = []

    def send(source, target):
        stores.append(pltpu.make_async_copy(source, target, leave.at[len(stores)]))
        stores[-1].start()

    for row in range(rows):
        part = stacked[:, row * columns : (row + 1) * columns]
        spreadout = lax.dot_general(part, pick, COLUMN_BY_COLUMN, preferred_element_type=F32)
        values = tokens[row].astype(F32) - spreadout[:, :channels]
        values = (values * spreadout[:, channels:] * gain).astype(BF)
        normed[row] = values
        planes[:, row * channels : (row + 1) * channels] = values
    send(normed, normed_hbm)
    send(normed.at[pl.ds(rows - margin, margin)], low_hbm)
    send(normed.at[pl.ds(0, margin)], high_hbm)
    inner = jnp.dot(table[...], planes[...], preferred_element_type=F32)
    total = None
    for row in range(rows):
        at = slice(row * channels, (row + 1) * channels)
        part = weights[:, at].astype(F32) * inner[:, at]
        total = part if total is None else total + part
    sampled_ref[...] = total.astype(BF)
    for store in stores:
        store.wait()


def normalize_and_sample(gain, corner_row, corner_col, fraction, tokens, moments):
    rows, columns, channels = tokens.shape
    points = corner_row.shape[0]
    vmem = pl.BlockSpec(memory_space=pltpu.VMEM)
    anywhere = pl.BlockSpec(memory_space=pl.ANY)
    edge = jax.ShapeDtypeStruct((KER // 2, columns, channels), BF)
    return pl.pallas_call(
        normalize_sample_kernel,
        in_specs=[vmem] * 4 + [anywhere] * 2,
        out_specs=(anywhere, anywhere, anywhere, vmem),
        out_shape=(
            jax.ShapeDtypeStruct(tokens.shape, BF),
            edge,
            edge,
            jax.ShapeDtypeStruct((points, channels), BF),
        ),
        scratch_shapes=[
            pltpu.VMEM(tokens.shape, BF),
            pltpu.VMEM(moments.shape, F32),
            pltpu.VMEM((points, columns), BF),
            pltpu.VMEM((points, rows * channels), BF),
            pltpu.VMEM(tokens.shape, BF),
            pltpu.VMEM((columns, rows * channels), BF),
            pltpu.SemaphoreType.DMA((2,)),
            pltpu.SemaphoreType.DMA((3,)),
        ],
        cost_estimate=pl.CostEstimate(flops=2 * 10**9, bytes_accessed=6 * 2**20, transcendentals=0),
        name="normalize_sample",
    )(
        gain,
        corner_row.reshape(1, points),
        corner_col.reshape(1, points),
        fraction,
        tokens,
        moments,
    )


def query_kernel(scale, groups, place_ref, *refs):
    row_refs, refs = refs[:groups], refs[groups:]
    gain_ref, own_ref, *rest = refs
    near_refs, far_refs, (out_ref,) = rest[: groups - 1], rest[groups - 1 : -1], rest[-1:]
    channels = row_refs[0].shape[1]
    width = groups * channels
    place, core = place_ref[0], place_ref[1]
    parts = [ref[...].astype(F32) for ref in row_refs]
    center = sum(jnp.sum(p, axis=1, keepdims=True) for p in parts) * (1.0 / width)
    parts = [p - center for p in parts]
    spread = sum(jnp.sum(jnp.square(p), axis=1, keepdims=True) for p in parts) * (1.0 / width)
    factor = lax.rsqrt(spread + EPS)
    normed, lines = [], []
    for distance, part in enumerate(parts):
        source = lax.rem(place + (groups - distance), groups)
        normed.append((part * factor * gain_ref[pl.ds(source, 1), :]).astype(BF))
        half = near_refs[0].shape[0]
        at = pl.multiple_of(source * channels, channels)
        inside = pl.ds(pl.multiple_of(lax.rem(at, half), channels), channels)
        mine = at // half == core
        line = [own_ref[pl.ds(at, channels), :]]
        for near, far in zip(near_refs, far_refs):
            line.append(jnp.where(mine, near[inside, :], far[inside, :]))
        lines.append(jnp.concatenate(line, axis=1))
    query = jnp.dot(
        jnp.concatenate(normed, axis=1),
        jnp.concatenate(lines, axis=0),
        preferred_element_type=F32,
    )
    for g in range(groups):
        out_ref[g] = (query[:, g * channels : (g + 1) * channels] * scale).astype(BF)


def weight_specs(which, groups, ahead, depth, channels):
    half = depth // 2
    own = pl.BlockSpec((None, depth, channels), lambda *_: (which, 0, 0))
    near = pl.BlockSpec((half, channels), lambda *_: (ahead // half + which, 0))
    far = pl.BlockSpec((half, channels), lambda *_: (which, 0))
    return [own, *[near] * (groups - 1), *[far] * (groups - 1)]


def query_of(place, row, gain, weights, columns, scale):
    own, near, far = weights
    groups = len(row)
    channels = own.shape[2]
    depth = own.shape[1]
    block = 256
    return pl.pallas_call(
        functools.partial(query_kernel, scale, groups),
        grid_spec=pltpu.PrefetchScalarGridSpec(
            num_scalar_prefetch=1,
            grid=(columns // block,),
            in_specs=[pl.BlockSpec((None, block, channels), lambda i, place: (place[0], i, 0))]
            + [pl.BlockSpec((block, channels), lambda i, place: (i, 0))] * (groups - 1)
            + [pl.BlockSpec(gain.shape, lambda i, place: (0, 0))]
            + weight_specs(0, groups, columns, depth, channels),
            out_specs=pl.BlockSpec((groups, block, channels), lambda i, place: (0, i, 0)),
        ),
        out_shape=jax.ShapeDtypeStruct((groups, columns, channels), BF),
        cost_estimate=pl.CostEstimate(flops=2 * 10**9, bytes_accessed=3 * 2**20, transcendentals=0),
        name="query",
    )(place, *row, gain, own, *near, *far)


def attend_kernel(per_group, first, start, block, place_ref, query_hbm, *refs):
    if first:
        blocks_hbm, own_hbm, *refs = refs
    else:
        key_hbm, value_hbm, own_hbm, *refs = refs
    groups, _, channels = query_hbm.shape
    others = groups - 1
    near_hbm, far_hbm, refs = refs[:others], refs[others : 2 * others], refs[2 * others :]
    if first:
        out_ref, key_hbm, value_hbm, query, keys, values, joined, arrive, leave, *refs = refs
        sampled, pairs = refs
    else:
        out_ref, query, keys, values, joined, arrive = refs
    core = place_ref[1]
    width = groups * channels
    half = width // 2
    count = query.shape[1]
    fetches = []

    def fetch(source, target):
        copy = pltpu.make_async_copy(source, target, arrive.at[len(fetches)])
        copy.start()
        fetches.append(copy)
        return copy

    def wait(copies):
        for copy in copies:
            copy.wait()

    def columns_of(g):
        return pl.ds(g * channels, channels)

    if first:
        gathered = [
            fetch(blocks_hbm.at[:, g], sampled.at[:, :, columns_of(g)]) for g in range(groups)
        ]
        paired = [
            [fetch(own_hbm.at[1 + side], pairs.at[0, :, columns_of(side)]) for side in range(2)]
        ]
        for g in range(1, groups):
            paired.append([])
            for side in range(2):
                for half_hbm, at in ((near_hbm[g - 1], core), (far_hbm[g - 1], 1 - core)):
                    lines = pl.ds(pl.multiple_of(at * half, half), half)
                    ahead = half_hbm.shape[0] - 4 * half
                    source = half_hbm.at[pl.ds(ahead + (1 + side) * half, half)]
                    paired[g].append(fetch(source, pairs.at[g, lines, columns_of(side)]))
    asked = fetch(query_hbm.at[:, pl.ds(start, count)], query)
    if not first:
        made = [
            [fetch(key_hbm.at[g], keys.at[g]), fetch(value_hbm.at[g], values.at[g])]
            for g in range(groups)
        ]
    joins = []
    for j in range(groups):
        source = own_hbm.at[3, columns_of(j)]
        joins.append(fetch(source, joined.at[columns_of(0), columns_of(j)]))
    per_half = groups // 2
    for g in range(1, groups):
        for j in range(per_half):
            for half_hbm, at in ((near_hbm[g - 1], core), (far_hbm[g - 1], 1 - core)):
                lanes = pl.ds(pl.multiple_of((at * per_half + j) * channels, channels), channels)
                ahead = half_hbm.shape[0] - half
                source = half_hbm.at[pl.ds(ahead + j * channels, channels)]
                joins.append(fetch(source, joined.at[columns_of(g), lanes]))

    if first:
        stores = []
        wait(gathered)
        points = sampled[...].reshape(keys.shape[1], width)
        for g in range(groups):
            wait(paired[g])
            product = jnp.dot(points, pairs[g], preferred_element_type=F32)
            keys[g] = product[:, :channels].astype(BF)
            values[g] = product[:, channels:].astype(BF)
        for source, target in ((keys, key_hbm), (values, value_hbm)):
            stores.append(pltpu.make_async_copy(source, target, leave.at[len(stores)]))
            stores[-1].start()

    else:
        for copies in made:
            wait(copies)
    asked.wait()
    wait(joins)
    head = lax.broadcasted_iota(jnp.int32, (1, channels), 1) // (channels // per_group)
    zero = jnp.zeros((), BF)
    one = jnp.ones((), BF)

    def one_block(index, carry):
        lines = pl.ds(pl.multiple_of(index * block, block), block)
        attended = []
        for g in range(groups):
            total = jnp.zeros((block, 2 * channels), F32)
            for h in range(per_group):
                key = jnp.where(head == h, keys[g], zero)
                scores = lax.dot_general(
                    query[g, lines, :], key, ROW_BY_ROW, preferred_element_type=F32
                )
                top = jnp.max(scores, axis=-1, keepdims=True)
                probs = jnp.exp2(scores - top).astype(BF)
                value = jnp.where(head == h, values[g], zero)
                ones = jnp.broadcast_to(jnp.where(head == h, one, zero), value.shape)
                both = jnp.concatenate([value, ones], axis=1)
                total = total + jnp.dot(probs, both, preferred_element_type=F32)
            attended.append((total[:, :channels] / total[:, channels:]).astype(BF))
        whole = jnp.concatenate(attended, axis=1)
        projected = jnp.dot(whole, joined[...], preferred_element_type=F32)
        for g in range(groups):
            out_ref[g, lines, :] = projected[:, g * channels : (g + 1) * channels].astype(BF)
        return carry

    lax.fori_loop(0, count // block, one_block, 0)
    if first:
        wait(stores)


def attend_and_project(place, query, source, weights, start, count, block):
    own, near, far = weights
    groups, _, channels = query.shape
    first = len(source) == 1
    width = groups * channels
    points = source[0].size // width
    vmem = pl.BlockSpec(memory_space=pltpu.VMEM)
    anywhere = pl.BlockSpec(memory_space=pl.ANY)
    out_specs, out_shape = vmem, jax.ShapeDtypeStruct((groups, count, channels), BF)
    operands = [query, *source, own, *near, *far]
    pair = (groups, points, channels)
    scratch = [
        pltpu.VMEM((groups, count, channels), BF),
        pltpu.VMEM(pair, BF),
        pltpu.VMEM(pair, BF),
        pltpu.VMEM((width, width), BF),
        pltpu.SemaphoreType.DMA((64,)),
    ]
    if first:
        made = jax.ShapeDtypeStruct(pair, BF)
        out_specs, out_shape = (vmem, anywhere, anywhere), (out_shape, made, made)
        bands, _, share, _ = source[0].shape
        scratch += [
            pltpu.SemaphoreType.DMA((2,)),
            pltpu.VMEM((bands, share, width), BF),
            pltpu.VMEM((groups, width, 2 * channels), BF),
        ]
    return pl.pallas_call(
        functools.partial(attend_kernel, HEADS // groups, first, start, block),
        in_specs=[pl.BlockSpec(memory_space=pltpu.SMEM)] + [anywhere] * len(operands),
        out_specs=out_specs,
        out_shape=out_shape,
        scratch_shapes=scratch,
        cost_estimate=pl.CostEstimate(
            flops=4 * count * points * width, bytes_accessed=4 * 2**20, transcendentals=0
        ),
        name="attend",
    )(place, *operands)


def convolve_kernel(
    low_ref, normed_ref, high_ref, tokens_ref, added_ref, taps_ref, mixed_ref, base_ref, padded
):
    rows, columns, channels = normed_ref.shape
    margin = KER // 2
    pad = 8
    step = pl.program_id(0)
    finished = pl.num_programs(0) // 2

    @pl.when(step == 0)
    def _():
        padded[:, 0:pad, :] = jnp.zeros((rows + 2 * margin, pad, channels), F32)
        padded[:, pad + columns :, :] = jnp.zeros((rows + 2 * margin, pad, channels), F32)
        padded[0:margin, pad : pad + columns, :] = low_ref[...].astype(F32)
        padded[margin : margin + rows, pad : pad + columns, :] = normed_ref[...].astype(F32)
        padded[margin + rows :, pad : pad + columns, :] = high_ref[...].astype(F32)

    taps = taps_ref[...]
    strip = 16
    span = tokens_ref.shape[1]
    begin = step * span

    def convolve_into(out_ref, added):
        def one_strip(index, carry):
            inside = pl.multiple_of(index * strip, strip)
            at = pl.ds(inside, strip)
            start = pl.multiple_of(begin + inside, strip)
            totals = [tokens_ref[r, at, :].astype(F32) for r in range(rows)]
            if added:
                totals = [t + added_ref[r, at, :].astype(F32) for r, t in enumerate(totals)]
            for second in range(KER):
                for line in range(rows + 2 * margin):
                    values = padded[line, pl.ds(start + pad - margin + second, strip), :]
                    for r in range(rows):
                        first = line - r
                        if 0 <= first < KER:
                            tap = first * KER + second
                            totals[r] = totals[r] + taps[tap : tap + 1, :] * values
            for r in range(rows):
                out_ref[r, at, :] = totals[r].astype(out_ref.dtype)
            return carry

        lax.fori_loop(0, span // strip, one_strip, 0)

    @pl.when(step < finished)
    def _():
        convolve_into(mixed_ref, True)

    @pl.when(step >= finished)
    def _():
        convolve_into(base_ref, False)


def convolve(low, normed, high, tokens, added, taps):
    rows, columns, channels = normed.shape
    steps = 4
    span = columns // steps
    last = steps // 2 - 1
    whole = pl.BlockSpec(normed.shape, lambda i: (0, 0, 0))
    piece = pl.BlockSpec((rows, span, channels), lambda i: (0, i, 0))
    front = pl.BlockSpec((rows, span, channels), lambda i: (0, jnp.minimum(i, last), 0))
    back = pl.BlockSpec((rows, span, channels), lambda i: (0, jnp.maximum(i - last - 1, 0), 0))
    edge = pl.BlockSpec(low.shape, lambda i: (0, 0, 0))
    return pl.pallas_call(
        convolve_kernel,
        grid=(steps,),
        in_specs=[edge, whole, edge, piece, front, pl.BlockSpec(taps.shape, lambda i: (0, 0))],
        out_specs=(front, back),
        out_shape=(
            jax.ShapeDtypeStruct(normed.shape, BF),
            jax.ShapeDtypeStruct((rows, columns // 2, channels), F32),
        ),
        scratch_shapes=[pltpu.VMEM((rows + 2 * (KER // 2), columns + 16, channels), F32)],
        cost_estimate=pl.CostEstimate(flops=10**9, bytes_accessed=6 * 2**20, transcendentals=0),
        name="convolve",
    )(low, normed, high, tokens, added, taps)


def body(
    tokens, corner_row, corner_col, fraction, w_query, w_key, w_value, w_out, conv_kernel, norm_gain
):
    _, columns, channels = tokens.shape
    groups = lax.axis_size("head")
    bands = lax.axis_size("band")
    width = groups * channels
    points = corner_row.shape[0]
    share = points // bands

    head = lax.axis_index("head")
    core = lax.axis_index("dp")
    place = jnp.stack([head, core])
    moments, own, bulk = moments_and_bulk(tokens, w_query, w_key, w_value, w_out, groups)
    moments = lax.all_to_all(moments, "head", 0, 0, tiled=True)

    def to_all_heads(blocks):
        arrived = {}
        for distance in (2, 1, 3):
            ring = [(i, (i + distance) % groups) for i in range(groups)]
            arrived[distance] = lax.ppermute(blocks[distance], "head", ring)
        return [arrived[distance] for distance in range(1, groups)]

    near = to_all_heads([None, *bulk])
    token_rows = [tokens, *near]
    far = [lax.ppermute(a[columns:], "dp", [(0, 1), (1, 0)]) for a in near]
    weights = (own, near, far)
    gain = norm_gain.reshape(groups, channels)

    normed, low, high, partial = normalize_and_sample(
        gain, corner_row, corner_col, fraction, tokens, moments
    )

    parts = lax.all_to_all(partial.reshape(bands, share, channels), "band", 0, 0, tiled=True)
    forward = [(i, i + 1) for i in range(bands - 1)]
    backward = [(target, source) for source, target in forward]
    low = lax.ppermute(low, "band", forward)
    high = lax.ppermute(high, "band", backward)
    piece = jnp.sum(parts.astype(F32), axis=0).astype(BF)
    copies = jnp.broadcast_to(piece, (bands * groups, *piece.shape))
    blocks = lax.all_to_all(copies, ("band", "head"), 0, 0, tiled=True)
    blocks = blocks.reshape(bands, groups, share, channels)

    size = width // HEADS
    scale = 1.4426950408889634 / size**0.5
    query = query_of(place, token_rows, gain, weights, columns, scale)
    half_way = columns // 2
    chunks = ((0, half_way, half_way), (half_way, half_way, half_way))
    returned = []
    source = (blocks,)
    for chunk, (start, count, block) in enumerate(chunks):
        projected = attend_and_project(place, query, source, weights, start, count, block)
        if chunk == 0:
            projected, *source = projected
        returned.append(lax.all_to_all(projected, "head", 0, 0, tiled=True))
    mixed, base = convolve(low, normed, high, tokens, returned[0], conv_kernel)
    rest = (base + returned[1].astype(F32)).astype(BF)
    return lax.dynamic_update_slice_in_dim(mixed, rest, half_way, 1)


def solution(mesh):
    return jax.shard_map(
        body,
        mesh=mesh,
        in_specs=(
            P(("dp", "band"), None, "head"),
            P("dp"),
            P("dp"),
            P(None, "dp"),
            P(None, "head"),
            P(None, "head"),
            P(None, "head"),
            P("head", None),
            P(None, "head"),
            P(),
        ),
        out_specs=P(("dp", "band"), None, "head"),
        check_vma=False,
    )
```

```python
import functools

import jax
import jax.numpy as jnp
from jax import lax
from jax.experimental import pallas as pl
from jax.experimental.pallas import tpu as pltpu
from jax.sharding import PartitionSpec as P


HEADS = 16
KER = 5
EPS = 1e-05
F32 = jnp.float32
BF = jnp.bfloat16
ROW_BY_ROW = (((1,), (1,)), ((), ()))
COLUMN_BY_COLUMN = (((0,), (0,)), ((), ()))


def split_in_three(x):
    high = x.astype(BF)
    rest = x - high.astype(F32)
    middle = rest.astype(BF)
    return high, middle, (rest - middle.astype(F32)).astype(BF)


def moments_kernel(
    tokens_hbm, query_hbm, key_hbm, value_hbm, out_weight_hbm, moments_ref, own_hbm, *refs
):
    *bulk_hbm, tokens_ref, own, half, arrive, leave = refs
    rows, columns, channels = tokens_ref.shape
    depth = query_hbm.shape[0]
    fetches = []

    def fetch(source, target):
        fetches.append(pltpu.make_async_copy(source, target, arrive.at[len(fetches)]))
        fetches[-1].start()

    for row in range(rows):
        fetch(tokens_hbm.at[row], tokens_ref.at[row])
    for index, source in enumerate((query_hbm, key_hbm, value_hbm)):
        fetch(source, own.at[index])
    for g in range(rows):
        at = pl.ds(g * channels, channels)
        fetch(out_weight_hbm.at[:, at], own.at[3, at])
    for waited in fetches:
        waited.wait()
    stores = []

    def send(source, target):
        stores.append(pltpu.make_async_copy(source, target, leave.at[len(stores)]))
        stores[-1].start()

    send(own, own_hbm)
    for distance, target in enumerate(bulk_hbm, 1):
        row = lax.rem(lax.axis_index("head") + distance, rows)
        send(tokens_ref.at[row], target.at[pl.ds(0, columns)])
    cut = depth // 2
    lines = pl.ds(pl.multiple_of(lax.axis_index("dp") * cut, cut), cut)
    for index in range(4):
        half[index * cut : (index + 1) * cut, :] = own[index, lines, :]
    for target in bulk_hbm:
        send(half, target.at[pl.ds(columns, 2 * depth)])
    side = lax.broadcasted_iota(jnp.int32, (8, 2 * channels), 1) // channels
    pick = jnp.where(side == lax.broadcasted_iota(jnp.int32, (8, 2 * channels), 0), 1.0, 0.0)
    pick = pick.astype(BF)
    average = jnp.full((channels, channels), 1.0 / channels, BF)
    for row in range(rows):
        block = tokens_ref[row]
        center = jnp.dot(block, average, preferred_element_type=F32)
        square = jnp.square(block.astype(F32) - center).astype(BF)
        both = jnp.concatenate([block, square], axis=1)
        facts = lax.dot_general(pick, both, ROW_BY_ROW, preferred_element_type=F32)
        at = pl.ds(row * columns, columns)
        for copy in range(moments_ref.shape[0]):
            moments_ref[copy, :, at] = facts[0:2]
    for store in stores:
        store.wait()


def moments_and_bulk(tokens, w_query, w_key, w_value, w_out, copies):
    rows, columns, channels = tokens.shape
    depth = w_query.shape[0]
    vmem = pl.BlockSpec(memory_space=pltpu.VMEM)
    anywhere = pl.BlockSpec(memory_space=pl.ANY)
    bulk = jax.ShapeDtypeStruct((columns + 2 * depth, channels), BF)
    moments, own, *bulk = pl.pallas_call(
        moments_kernel,
        in_specs=[anywhere] * 5,
        out_specs=(vmem, anywhere, *[anywhere] * (copies - 1)),
        out_shape=(
            jax.ShapeDtypeStruct((copies, 2, rows * columns), F32),
            jax.ShapeDtypeStruct((4, depth, channels), BF),
            *[bulk] * (copies - 1),
        ),
        scratch_shapes=[
            pltpu.VMEM(tokens.shape, BF),
            pltpu.VMEM((4, depth, channels), BF),
            pltpu.VMEM((2 * depth, channels), BF),
            pltpu.SemaphoreType.DMA((2 * rows + 3,)),
            pltpu.SemaphoreType.DMA((2 * copies - 1,)),
        ],
        cost_estimate=pl.CostEstimate(flops=10**9, bytes_accessed=2**20, transcendentals=0),
        name="moments",
    )(tokens, w_query, w_key, w_value, w_out)
    return moments, own, bulk


def make_tables(band, row_ref, column_ref, fraction_ref, table_ref, weight_ref):
    _, columns = table_ref.shape
    rows = weight_ref.shape[1] // 128
    lines = row_ref[...]
    start = band * rows
    column = column_ref[...]
    vertical = fraction_ref[0:1, :]
    horizontal = fraction_ref[1:2, :]
    top = (1.0 - vertical).astype(BF).astype(F32)
    bottom = vertical.astype(BF).astype(F32)
    coarse = (column // 8) * 8
    facts = [
        coarse.astype(F32),
        (column - coarse).astype(F32),
        (1.0 - horizontal).astype(BF).astype(F32),
        horizontal.astype(BF).astype(F32),
    ]
    for r in range(rows):
        here = jnp.where(lines == start + r, top, 0.0)
        facts.append(here + jnp.where(lines + 1 == start + r, bottom, 0.0))
    facts += [jnp.zeros_like(facts[0])] * (16 - len(facts))
    facts = jnp.concatenate(facts, axis=0).astype(BF)
    kinds = 3 + rows
    fact = lax.broadcasted_iota(jnp.int32, (16, kinds * 128), 0)
    kind = lax.broadcasted_iota(jnp.int32, (16, kinds * 128), 1) // 128
    pick = (jnp.maximum(fact - 1, 0) == kind) & (fact < kinds + 1)
    spread = lax.dot_general(
        facts,
        jnp.where(pick, 1.0, 0.0).astype(BF),
        COLUMN_BY_COLUMN,
        preferred_element_type=F32,
    )
    weight_ref[...] = spread[:, 3 * 128 :].astype(BF)
    middle = spread[:, :128]
    left, right = spread[:, 128:256], spread[:, 256:384]
    lane = lax.broadcasted_iota(jnp.int32, (1, 128), 1).astype(F32)
    for block in range(columns // 128):
        offset = lane + float(block * 128) - middle
        values = jnp.where(offset == 0.0, left, jnp.where(offset == 1.0, right, 0.0))
        table_ref[:, block * 128 : (block + 1) * 128] = values.astype(BF)


def normalize_sample_kernel(
    gain_ref,
    row_ref,
    column_ref,
    fraction_ref,
    tokens_hbm,
    moments_hbm,
    normed_hbm,
    low_hbm,
    high_hbm,
    sampled_ref,
    tokens,
    moments,
    table,
    weights,
    normed,
    planes,
    arrive,
    leave,
):
    fetches = []
    for index, (source, target) in enumerate(
        ((moments_hbm, moments), (tokens_hbm, tokens))
    ):
        fetches.append(pltpu.make_async_copy(source, target, arrive.at[index]))
        fetches[-1].start()
    rows, columns, channels = tokens.shape
    devices = moments.shape[0]
    make_tables(lax.axis_index("band"), row_ref, column_ref, fraction_ref, table, weights)
    fetches[0].wait()
    sums = [moments[d, 0:1, :] for d in range(devices)]
    width = channels * devices
    center = functools.reduce(jnp.add, sums) * (1.0 / width)
    spread = functools.reduce(jnp.add, [moments[d, 1:2, :] for d in range(devices)])
    for d in range(devices):
        spread = spread + channels * jnp.square(sums[d] * (1.0 / channels) - center)
    factor = lax.rsqrt(spread * (1.0 / width) + EPS)
    pieces = [*split_in_three(center), *split_in_three(factor)]
    pieces += [jnp.zeros_like(pieces[0])] * 10
    stacked = jnp.concatenate([p.astype(F32) for p in pieces], axis=0).astype(BF)
    piece = lax.broadcasted_iota(jnp.int32, (16, 2 * channels), 0)
    lane = lax.broadcasted_iota(jnp.int32, (16, 2 * channels), 1)
    pick = jnp.where((piece < 6) & (piece // 3 == lane // channels), 1.0, 0.0).astype(BF)
    gain = gain_ref[pl.ds(lax.axis_index("head"), 1), :]
    margin = KER // 2
    fetches[1].wait()
    stores = []

    def send(source, target):
        stores.append(pltpu.make_async_copy(source, target, leave.at[len(stores)]))
        stores[-1].start()

    for row in range(rows):
        part = stacked[:, row * columns : (row + 1) * columns]
        spreadout = lax.dot_general(part, pick, COLUMN_BY_COLUMN, preferred_element_type=F32)
        values = tokens[row].astype(F32) - spreadout[:, :channels]
        values = (values * spreadout[:, channels:] * gain).astype(BF)
        normed[row] = values
        planes[:, row * channels : (row + 1) * channels] = values
    send(normed, normed_hbm)
    send(normed.at[pl.ds(rows - margin, margin)], low_hbm)
    send(normed.at[pl.ds(0, margin)], high_hbm)
    inner = jnp.dot(table[...], planes[...], preferred_element_type=F32)
    total = None
    for row in range(rows):
        at = slice(row * channels, (row + 1) * channels)
        part = weights[:, at].astype(F32) * inner[:, at]
        total = part if total is None else total + part
    sampled_ref[...] = total.astype(BF)
    for store in stores:
        store.wait()


def normalize_and_sample(gain, corner_row, corner_col, fraction, tokens, moments):
    rows, columns, channels = tokens.shape
    points = corner_row.shape[0]
    vmem = pl.BlockSpec(memory_space=pltpu.VMEM)
    anywhere = pl.BlockSpec(memory_space=pl.ANY)
    edge = jax.ShapeDtypeStruct((KER // 2, columns, channels), BF)
    return pl.pallas_call(
        normalize_sample_kernel,
        in_specs=[vmem] * 4 + [anywhere] * 2,
        out_specs=(anywhere, anywhere, anywhere, vmem),
        out_shape=(
            jax.ShapeDtypeStruct(tokens.shape, BF),
            edge,
            edge,
            jax.ShapeDtypeStruct((points, channels), BF),
        ),
        scratch_shapes=[
            pltpu.VMEM(tokens.shape, BF),
            pltpu.VMEM(moments.shape, F32),
            pltpu.VMEM((points, columns), BF),
            pltpu.VMEM((points, rows * channels), BF),
            pltpu.VMEM(tokens.shape, BF),
            pltpu.VMEM((columns, rows * channels), BF),
            pltpu.SemaphoreType.DMA((2,)),
            pltpu.SemaphoreType.DMA((3,)),
        ],
        cost_estimate=pl.CostEstimate(flops=2 * 10**9, bytes_accessed=6 * 2**20, transcendentals=0),
        name="normalize_sample",
    )(
        gain,
        corner_row.reshape(1, points),
        corner_col.reshape(1, points),
        fraction,
        tokens,
        moments,
    )


def query_kernel(scale, groups, place_ref, *refs):
    row_refs, refs = refs[:groups], refs[groups:]
    gain_ref, own_ref, *rest = refs
    near_refs, far_refs, (out_ref,) = rest[: groups - 1], rest[groups - 1 : -1], rest[-1:]
    channels = row_refs[0].shape[1]
    width = groups * channels
    place, core = place_ref[0], place_ref[1]
    parts = [ref[...].astype(F32) for ref in row_refs]
    center = sum(jnp.sum(p, axis=1, keepdims=True) for p in parts) * (1.0 / width)
    parts = [p - center for p in parts]
    spread = sum(jnp.sum(jnp.square(p), axis=1, keepdims=True) for p in parts) * (1.0 / width)
    factor = lax.rsqrt(spread + EPS)
    normed, lines = [], []
    for distance, part in enumerate(parts):
        source = lax.rem(place + (groups - distance), groups)
        normed.append((part * factor * gain_ref[pl.ds(source, 1), :]).astype(BF))
        half = near_refs[0].shape[0]
        at = pl.multiple_of(source * channels, channels)
        inside = pl.ds(pl.multiple_of(lax.rem(at, half), channels), channels)
        mine = at // half == core
        line = [own_ref[pl.ds(at, channels), :]]
        for near, far in zip(near_refs, far_refs):
            line.append(jnp.where(mine, near[inside, :], far[inside, :]))
        lines.append(jnp.concatenate(line, axis=1))
    query = jnp.dot(
        jnp.concatenate(normed, axis=1),
        jnp.concatenate(lines, axis=0),
        preferred_element_type=F32,
    )
    for g in range(groups):
        out_ref[g] = (query[:, g * channels : (g + 1) * channels] * scale).astype(BF)


def weight_specs(which, groups, ahead, depth, channels):
    half = depth // 2
    own = pl.BlockSpec((None, depth, channels), lambda *_: (which, 0, 0))
    near = pl.BlockSpec((half, channels), lambda *_: (ahead // half + which, 0))
    far = pl.BlockSpec((half, channels), lambda *_: (which, 0))
    return [own, *[near] * (groups - 1), *[far] * (groups - 1)]


def query_of(place, row, gain, weights, columns, scale):
    own, near, far = weights
    groups = len(row)
    channels = own.shape[2]
    depth = own.shape[1]
    block = 256
    return pl.pallas_call(
        functools.partial(query_kernel, scale, groups),
        grid_spec=pltpu.PrefetchScalarGridSpec(
            num_scalar_prefetch=1,
            grid=(columns // block,),
            in_specs=[pl.BlockSpec((None, block, channels), lambda i, place: (place[0], i, 0))]
            + [pl.BlockSpec((block, channels), lambda i, place: (i, 0))] * (groups - 1)
            + [pl.BlockSpec(gain.shape, lambda i, place: (0, 0))]
            + weight_specs(0, groups, columns, depth, channels),
            out_specs=pl.BlockSpec((groups, block, channels), lambda i, place: (0, i, 0)),
        ),
        out_shape=jax.ShapeDtypeStruct((groups, columns, channels), BF),
        cost_estimate=pl.CostEstimate(flops=2 * 10**9, bytes_accessed=3 * 2**20, transcendentals=0),
        name="query",
    )(place, *row, gain, own, *near, *far)


def attend_kernel(per_group, first, start, block, place_ref, query_hbm, *refs):
    if first:
        blocks_hbm, own_hbm, *refs = refs
    else:
        key_hbm, value_hbm, own_hbm, *refs = refs
    groups, _, channels = query_hbm.shape
    others = groups - 1
    near_hbm, far_hbm, refs = refs[:others], refs[others : 2 * others], refs[2 * others :]
    if first:
        out_ref, key_hbm, value_hbm, query, keys, values, joined, arrive, leave, *refs = refs
        sampled, pairs = refs
    else:
        out_ref, query, keys, values, joined, arrive = refs
    core = place_ref[1]
    width = groups * channels
    half = width // 2
    count = query.shape[1]
    fetches = []

    def fetch(source, target):
        copy = pltpu.make_async_copy(source, target, arrive.at[len(fetches)])
        copy.start()
        fetches.append(copy)
        return copy

    def wait(copies):
        for copy in copies:
            copy.wait()

    def columns_of(g):
        return pl.ds(g * channels, channels)

    if first:
        gathered = [
            fetch(blocks_hbm.at[:, g], sampled.at[:, :, columns_of(g)]) for g in range(groups)
        ]
        paired = [
            [fetch(own_hbm.at[1 + side], pairs.at[0, :, columns_of(side)]) for side in range(2)]
        ]
        for g in range(1, groups):
            paired.append([])
            for side in range(2):
                for half_hbm, at in ((near_hbm[g - 1], core), (far_hbm[g - 1], 1 - core)):
                    lines = pl.ds(pl.multiple_of(at * half, half), half)
                    ahead = half_hbm.shape[0] - 4 * half
                    source = half_hbm.at[pl.ds(ahead + (1 + side) * half, half)]
                    paired[g].append(fetch(source, pairs.at[g, lines, columns_of(side)]))
    asked = fetch(query_hbm.at[:, pl.ds(start, count)], query)
    if not first:
        made = [
            [fetch(key_hbm.at[g], keys.at[g]), fetch(value_hbm.at[g], values.at[g])]
            for g in range(groups)
        ]
    joins = []
    for j in range(groups):
        source = own_hbm.at[3, columns_of(j)]
        joins.append(fetch(source, joined.at[columns_of(0), columns_of(j)]))
    per_half = groups // 2
    for g in range(1, groups):
        for j in range(per_half):
            for half_hbm, at in ((near_hbm[g - 1], core), (far_hbm[g - 1], 1 - core)):
                lanes = pl.ds(pl.multiple_of((at * per_half + j) * channels, channels), channels)
                ahead = half_hbm.shape[0] - half
                source = half_hbm.at[pl.ds(ahead + j * channels, channels)]
                joins.append(fetch(source, joined.at[columns_of(g), lanes]))

    if first:
        stores = []
        wait(gathered)
        points = sampled[...].reshape(keys.shape[1], width)
        for g in range(groups):
            wait(paired[g])
            product = jnp.dot(points, pairs[g], preferred_element_type=F32)
            keys[g] = product[:, :channels].astype(BF)
            values[g] = product[:, channels:].astype(BF)
        for source, target in ((keys, key_hbm), (values, value_hbm)):
            stores.append(pltpu.make_async_copy(source, target, leave.at[len(stores)]))
            stores[-1].start()

    else:
        for copies in made:
            wait(copies)
    asked.wait()
    wait(joins)
    head = lax.broadcasted_iota(jnp.int32, (1, channels), 1) // (channels // per_group)
    zero = jnp.zeros((), BF)
    one = jnp.ones((), BF)

    def one_block(index, carry):
        lines = pl.ds(pl.multiple_of(index * block, block), block)
        attended = []
        for g in range(groups):
            total = jnp.zeros((block, 2 * channels), F32)
            for h in range(per_group):
                key = jnp.where(head == h, keys[g], zero)
                scores = lax.dot_general(
                    query[g, lines, :], key, ROW_BY_ROW, preferred_element_type=F32
                )
                top = jnp.max(scores, axis=-1, keepdims=True)
                probs = jnp.exp2(scores - top).astype(BF)
                value = jnp.where(head == h, values[g], zero)
                ones = jnp.broadcast_to(jnp.where(head == h, one, zero), value.shape)
                both = jnp.concatenate([value, ones], axis=1)
                total = total + jnp.dot(probs, both, preferred_element_type=F32)
            attended.append((total[:, :channels] / total[:, channels:]).astype(BF))
        whole = jnp.concatenate(attended, axis=1)
        projected = jnp.dot(whole, joined[...], preferred_element_type=F32)
        for g in range(groups):
            out_ref[g, lines, :] = projected[:, g * channels : (g + 1) * channels].astype(BF)
        return carry

    lax.fori_loop(0, count // block, one_block, 0)
    if first:
        wait(stores)


def attend_and_project(place, query, source, weights, start, count, block):
    own, near, far = weights
    groups, _, channels = query.shape
    first = len(source) == 1
    width = groups * channels
    points = source[0].size // width
    vmem = pl.BlockSpec(memory_space=pltpu.VMEM)
    anywhere = pl.BlockSpec(memory_space=pl.ANY)
    out_specs, out_shape = vmem, jax.ShapeDtypeStruct((groups, count, channels), BF)
    operands = [query, *source, own, *near, *far]
    pair = (groups, points, channels)
    scratch = [
        pltpu.VMEM((groups, count, channels), BF),
        pltpu.VMEM(pair, BF),
        pltpu.VMEM(pair, BF),
        pltpu.VMEM((width, width), BF),
        pltpu.SemaphoreType.DMA((64,)),
    ]
    if first:
        made = jax.ShapeDtypeStruct(pair, BF)
        out_specs, out_shape = (vmem, anywhere, anywhere), (out_shape, made, made)
        bands, _, share, _ = source[0].shape
        scratch += [
            pltpu.SemaphoreType.DMA((2,)),
            pltpu.VMEM((bands, share, width), BF),
            pltpu.VMEM((groups, width, 2 * channels), BF),
        ]
    return pl.pallas_call(
        functools.partial(attend_kernel, HEADS // groups, first, start, block),
        in_specs=[pl.BlockSpec(memory_space=pltpu.SMEM)] + [anywhere] * len(operands),
        out_specs=out_specs,
        out_shape=out_shape,
        scratch_shapes=scratch,
        cost_estimate=pl.CostEstimate(
            flops=4 * count * points * width, bytes_accessed=4 * 2**20, transcendentals=0
        ),
        name="attend",
    )(place, *operands)


def convolve_kernel(low_ref, normed_ref, high_ref, tokens_ref, taps_ref, out_ref, padded):
    rows, columns, channels = normed_ref.shape
    margin = KER // 2
    pad = 8

    @pl.when(pl.program_id(0) == 0)
    def _():
        padded[:, 0:pad, :] = jnp.zeros((rows + 2 * margin, pad, channels), F32)
        padded[:, pad + columns :, :] = jnp.zeros((rows + 2 * margin, pad, channels), F32)
        padded[0:margin, pad : pad + columns, :] = low_ref[...].astype(F32)
        padded[margin : margin + rows, pad : pad + columns, :] = normed_ref[...].astype(F32)
        padded[margin + rows :, pad : pad + columns, :] = high_ref[...].astype(F32)

    taps = taps_ref[...]
    strip = 16
    span = tokens_ref.shape[1]
    begin = pl.program_id(0) * span

    def one_strip(index, carry):
        inside = pl.multiple_of(index * strip, strip)
        start = pl.multiple_of(begin + inside, strip)
        totals = [tokens_ref[r, pl.ds(inside, strip), :].astype(F32) for r in range(rows)]
        for second in range(KER):
            for line in range(rows + 2 * margin):
                values = padded[line, pl.ds(start + pad - margin + second, strip), :]
                for r in range(rows):
                    first = line - r
                    if 0 <= first < KER:
                        tap = first * KER + second
                        totals[r] = totals[r] + taps[tap : tap + 1, :] * values
        for r in range(rows):
            out_ref[r, pl.ds(inside, strip), :] = totals[r]
        return carry

    lax.fori_loop(0, span // strip, one_strip, 0)


def convolve(low, normed, high, tokens, taps):
    rows, columns, channels = normed.shape
    span = columns // 4
    piece = pl.BlockSpec((rows, span, channels), lambda i: (0, i, 0))
    edge = pl.BlockSpec(low.shape, lambda i: (0, 0, 0))
    return pl.pallas_call(
        convolve_kernel,
        grid=(columns // span,),
        in_specs=[
            edge,
            pl.BlockSpec(normed.shape, lambda i: (0, 0, 0)),
            edge,
            piece,
            pl.BlockSpec(taps.shape, lambda i: (0, 0)),
        ],
        out_specs=piece,
        out_shape=jax.ShapeDtypeStruct(normed.shape, F32),
        scratch_shapes=[pltpu.VMEM((rows + 2 * (KER // 2), columns + 16, channels), F32)],
        cost_estimate=pl.CostEstimate(flops=10**9, bytes_accessed=6 * 2**20, transcendentals=0),
        name="convolve",
    )(low, normed, high, tokens, taps)


def body(
    tokens, corner_row, corner_col, fraction, w_query, w_key, w_value, w_out, conv_kernel, norm_gain
):
    _, columns, channels = tokens.shape
    groups = lax.axis_size("head")
    bands = lax.axis_size("band")
    width = groups * channels
    points = corner_row.shape[0]
    share = points // bands

    head = lax.axis_index("head")
    core = lax.axis_index("dp")
    place = jnp.stack([head, core])
    moments, own, bulk = moments_and_bulk(tokens, w_query, w_key, w_value, w_out, groups)
    moments = lax.all_to_all(moments, "head", 0, 0, tiled=True)

    def to_all_heads(blocks):
        arrived = {}
        for distance in (2, 1, 3):
            ring = [(i, (i + distance) % groups) for i in range(groups)]
            arrived[distance] = lax.ppermute(blocks[distance], "head", ring)
        return [arrived[distance] for distance in range(1, groups)]

    near = to_all_heads([None, *bulk])
    token_rows = [tokens, *near]
    far = [lax.ppermute(a[columns:], "dp", [(0, 1), (1, 0)]) for a in near]
    weights = (own, near, far)
    gain = norm_gain.reshape(groups, channels)

    normed, low, high, partial = normalize_and_sample(
        gain, corner_row, corner_col, fraction, tokens, moments
    )

    parts = lax.all_to_all(partial.reshape(bands, share, channels), "band", 0, 0, tiled=True)
    forward = [(i, i + 1) for i in range(bands - 1)]
    backward = [(target, source) for source, target in forward]
    low = lax.ppermute(low, "band", forward)
    high = lax.ppermute(high, "band", backward)
    piece = jnp.sum(parts.astype(F32), axis=0).astype(BF)
    copies = jnp.broadcast_to(piece, (bands * groups, *piece.shape))
    blocks = lax.all_to_all(copies, ("band", "head"), 0, 0, tiled=True)
    blocks = blocks.reshape(bands, groups, share, channels)

    size = width // HEADS
    scale = 1.4426950408889634 / size**0.5
    query = query_of(place, token_rows, gain, weights, columns, scale)
    cut = 5 * columns // 8
    chunks = ((0, cut, cut), (cut, columns - cut, columns - cut))
    returned = []
    source = (blocks,)
    for chunk, (start, count, block) in enumerate(chunks):
        projected = attend_and_project(place, query, source, weights, start, count, block)
        if chunk == 0:
            projected, *source = projected
        returned.append(lax.all_to_all(projected, "head", 0, 0, tiled=True))
    base = convolve(low, normed, high, tokens, conv_kernel)
    projected = jnp.concatenate(returned, axis=1)
    return (base + projected.astype(F32)).astype(BF)


def solution(mesh):
    return jax.shard_map(
        body,
        mesh=mesh,
        in_specs=(
            P(("dp", "band"), None, "head"),
            P("dp"),
            P("dp"),
            P(None, "dp"),
            P(None, "head"),
            P(None, "head"),
            P(None, "head"),
            P("head", None),
            P(None, "head"),
            P(),
        ),
        out_specs=P(("dp", "band"), None, "head"),
        check_vma=False,
    )
```
